256 devices in a mesh: ctx: 32 (over y_lo, z, core), tp: 8 (over x, y_hi).
Axes of the slice: x: 4, y: 4 (y_hi: 2, y_lo: 2; y = y_hi * 2 + y_lo), z: 8, core: 2. Of those that a mesh axis runs over, the one named last changes fastest.
Arguments:
- queries: bfloat16 [16384, 4096], P('ctx', 'tp'), may hold values from -5 to 5
- keys: bfloat16 [16384, 4096], P('ctx', 'tp'), may hold values from -5 to 5
- values: bfloat16 [16384, 4096], P('ctx', 'tp'), may hold values from -21 to 21
- log_decay: float32 [32, 16384], P('tp', 'ctx'), may hold values from -0.7 to 0
- gate: bfloat16 [16384, 4096], P('ctx', 'tp'), may hold values from -6 to 6
- gain: float32 [4096], P('tp'), may hold values from 0.5 to 1.5
- grad_out: bfloat16 [16384, 4096], P(('ctx', 'tp')), may hold values from -20 to 20
Outputs:
- query_grad: bfloat16 [16384, 4096], P('ctx', 'tp')
- key_grad: bfloat16 [16384, 4096], P('ctx', 'tp')
- value_grad: bfloat16 [16384, 4096], P('ctx', 'tp')
- gate_grad: bfloat16 [16384, 4096], P('ctx', 'tp')
- gain_grad: float32 [4096], P('tp')
The draws below stay inside these ranges and needn't reach their ends.
All inputs are finite; a program needn't handle non-finite values.
Results may differ from the reference program's by a relative error of at most 0.005.
Values may be sent and summed in bfloat16 or wider, within the bound.
A program may use at most 64 MiB of HBM per device.

```python
import math
import jax
import jax.numpy as jnp
from jax import lax

HEAD = 128
HEADS = 32
BLOCK = 512
TOKEN_POSITIONS = 16384
HD_ALL = 4096


def draw_log_decay(key, part):
    sequence_lanes = jax.random.split(key, 6)
    fraction = 0.5
    is_fast = jax.random.uniform(sequence_lanes[0], (HEADS, 1), jnp.float32) < fraction
    fast_rate = jnp.exp(jax.random.uniform(sequence_lanes[1], (HEADS, 1), jnp.float32, minval=math.log(1.0 / 50.0), maxval=math.log(1.0 / 30.0)))
    slow_rate = jnp.exp(jax.random.uniform(sequence_lanes[2], (HEADS, 1), jnp.float32, minval=math.log(0.1), maxval=0.0)) / TOKEN_POSITIONS
    head_forget_rate = jnp.where(is_fast, fast_rate, slow_rate)
    segments = (TOKEN_POSITIONS + 127) // 128
    decay_factor = jnp.exp(jax.random.uniform(sequence_lanes[3], (HEADS, segments), jnp.float32, minval=-0.7, maxval=0.7))
    decay_factor = jnp.repeat(decay_factor, 128, axis=1)[:, :TOKEN_POSITIONS]
    grouped_segments = jax.random.uniform(sequence_lanes[4], (1, TOKEN_POSITIONS), jnp.float32) < 3.0 / TOKEN_POSITIONS
    excluded_terms = jnp.log(jax.random.uniform(sequence_lanes[5], (1, TOKEN_POSITIONS), jnp.float32, minval=0.5, maxval=0.8))
    return jnp.where(grouped_segments, excluded_terms, -head_forget_rate * decay_factor)


def draw_values(key, part):
    sequence_lanes = jax.random.split(key, 1)
    head_index = (jnp.arange(HEADS * HEAD) // HEAD).astype(jnp.float32)
    spread = 1.0 + 2.0 * head_index / (HEADS - 1)
    base = jnp.clip(jax.random.normal(sequence_lanes[0], (TOKEN_POSITIONS, HEADS * HEAD), jnp.float32), -5.0, 5.0)
    return (base * spread[None, :]).astype(jnp.bfloat16)


def draw_grad_out(key, part):
    sequence_lanes = jax.random.split(key, 1)
    position = jnp.arange(TOKEN_POSITIONS).astype(jnp.float32) / (TOKEN_POSITIONS - 1)
    rising = (1.0 + 2.0 * position)[:, None]
    base = jnp.clip(jax.random.normal(sequence_lanes[0], (TOKEN_POSITIONS, HEADS * HEAD), jnp.float32), -5.0, 5.0)
    return (base * rising).astype(jnp.bfloat16)


def levels(key, shape, shards, least, largest):
    def one(dim, shards_of):
        steps = jax.random.uniform(jax.random.fold_in(jax.random.fold_in(key, 6), dim), (shards_of,), jnp.float32, least / len(shards), largest / len(shards))
        return jnp.repeat(jnp.exp(steps), shape[dim] // shards_of).reshape((-1,) + (1,) * (len(shape) - dim - 1))

    level = one(*shards[0])
    for cut in shards[1:]:
        level = level * one(*cut)
    return level


def scatter_about(stream_key, shape, deviation, reach, cuts=(), kind=jnp.bfloat16):
    entries = deviation * jax.random.normal(stream_key, shape, jnp.float32)
    if cuts:
        entries = entries * levels(stream_key, shape, cuts, -0.22, 0.18)
    return jnp.clip(entries, -reach, reach).astype(kind)


def setup_inputs(seed: int = 0) -> dict:
    arg_keys = jax.random.split(jax.random.key(seed), 8)
    queries = scatter_about(arg_keys[0], (TOKEN_POSITIONS, HD_ALL), 1.0, 5.0, ((0, 32), (1, 8)))
    keys = scatter_about(arg_keys[1], (TOKEN_POSITIONS, HD_ALL), 1.0, 5.0, ((0, 32), (1, 8)))
    values = draw_values(jax.random.fold_in(arg_keys[7], 71), 0)
    log_decay = draw_log_decay(jax.random.fold_in(arg_keys[7], 71), 0)
    gate = scatter_about(arg_keys[4], (TOKEN_POSITIONS, HD_ALL), 1.5, 6.0, ((0, 32), (1, 8)))
    gain = jnp.clip(1.0 + 0.1 * jax.random.normal(arg_keys[5], (HD_ALL,), jnp.float32), 0.5, 1.5)
    grad_out = draw_grad_out(jax.random.fold_in(arg_keys[7], 71), 0)
    return {"queries": queries, "keys": keys, "values": values, "log_decay": log_decay, "gate": gate, "gain": gain, "grad_out": grad_out}


HIGH_PRECISION = lax.Precision.HIGHEST
EPSILON = 1e-06

def decay_mask(decay_block):
    by_head = jnp.transpose(decay_block, (1, 0))
    spread = by_head[:, :, None] - by_head[:, None, :]
    causal = jnp.tril(jnp.ones((BLOCK, BLOCK), dtype=bool))
    return jnp.where(causal[None], jnp.exp(jnp.minimum(spread, 0.0)), 0.0)

def block_forward(carried_state, element):
    query_block, key_block, value_block, decay_block = element
    full_query_rows = query_block.astype(jnp.float32)
    full_key_rows = key_block.astype(jnp.float32)
    full_value_rows = value_block.astype(jnp.float32)
    block_decay_rate = decay_block[-1]
    table = decay_mask(decay_block)
    attention_scores = jnp.einsum('rgs,fgs->grf', full_query_rows, full_key_rows)
    probs = lax.optimization_barrier((attention_scores * table).astype(jnp.bfloat16))
    intra = jnp.einsum('hlm,mhe->lhe', probs.astype(jnp.float32), full_value_rows)
    growth = jnp.exp(decay_block)[:, :, None]
    decay_shrink = jnp.exp(block_decay_rate[None, :] - decay_block)[:, :, None]
    inter = jnp.einsum('lhd,hde->lhe', full_query_rows * growth, carried_state, precision=HIGH_PRECISION)
    addend = jnp.einsum('lhd,lhe->hde', full_key_rows * decay_shrink, full_value_rows, precision=HIGH_PRECISION)
    updated = jnp.exp(block_decay_rate)[:, None, None] * carried_state + addend
    return (updated, (intra + inter, carried_state))

def block_backward(carried_state, element):
    query_block, key_block, value_block, decay_block, dattn_block, prev_state = element
    full_query_rows = query_block.astype(jnp.float32)
    full_key_rows = key_block.astype(jnp.float32)
    full_value_rows = value_block.astype(jnp.float32)
    wide_dattn = dattn_block.astype(jnp.float32)
    block_decay_rate = decay_block[-1]
    table = decay_mask(decay_block)
    attention_scores = jnp.einsum('rgs,fgs->grf', full_query_rows, full_key_rows)
    probs = lax.optimization_barrier((attention_scores * table).astype(jnp.bfloat16)).astype(jnp.float32)
    dprobs = jnp.einsum('lhe,mhe->hlm', wide_dattn, full_value_rows)
    scores_gradient = lax.optimization_barrier((dprobs * table).astype(jnp.bfloat16)).astype(jnp.float32)
    growth = jnp.exp(decay_block)[:, :, None]
    decay_shrink = jnp.exp(block_decay_rate[None, :] - decay_block)[:, :, None]
    query_portion = jnp.einsum('fxz,zfb->xfb', scores_gradient, full_key_rows)
    query_portion = query_portion + jnp.einsum('lhe,hde->lhd', wide_dattn * growth, prev_state, precision=HIGH_PRECISION)
    key_portion = jnp.einsum('fzu,zfj->ufj', scores_gradient, full_query_rows)
    key_portion = key_portion + jnp.einsum('bip,iup->biu', full_value_rows * decay_shrink, carried_state, precision=HIGH_PRECISION)
    value_portion = jnp.einsum('hlm,lhe->mhe', probs, wide_dattn)
    value_portion = value_portion + jnp.einsum('bfj,fjq->bfq', full_key_rows * decay_shrink, carried_state, precision=HIGH_PRECISION)
    backterm = jnp.einsum('lhd,lhe->hde', full_query_rows * growth, wide_dattn, precision=HIGH_PRECISION)
    updated = jnp.exp(block_decay_rate)[:, None, None] * carried_state + backterm
    return (updated, (query_portion.astype(jnp.bfloat16), key_portion.astype(jnp.bfloat16), value_portion.astype(jnp.bfloat16)))

def reference(queries, keys, values, log_decay, gate, gain, grad_out):
    count = TOKEN_POSITIONS // BLOCK
    shape4 = (count, BLOCK, HEADS, HEAD)
    query_blocks = queries.reshape(shape4)
    key_blocks = keys.reshape(shape4)
    value_blocks = values.reshape(shape4)
    rates = jnp.transpose(log_decay.reshape(HEADS, count, BLOCK), (1, 2, 0))
    decay_sum = jnp.cumsum(rates, axis=1)
    start = jnp.zeros((HEADS, HEAD, HEAD), jnp.float32)
    _, (attention, prev_states) = lax.scan(block_forward, start, (query_blocks, key_blocks, value_blocks, decay_sum))
    gate_blocks = gate.reshape(shape4).astype(jnp.float32)
    grad_blocks = grad_out.reshape(shape4).astype(jnp.float32)
    gain_heads = gain.reshape(HEADS, HEAD)
    opened = jax.nn.sigmoid(gate_blocks)
    dnorm = grad_blocks * opened
    dscaled = dnorm * gain_heads
    squares = lax.optimization_barrier(jnp.sum(attention * attention, axis=(2, 3)))
    inner = lax.optimization_barrier(jnp.sum(attention * dscaled, axis=(2, 3)))
    rscale = lax.rsqrt(squares / (HEADS * HEAD) + EPSILON)[:, :, None, None]
    normed = attention * rscale * gain_heads
    gate_grad = (grad_blocks * normed * opened * (1.0 - opened)).astype(jnp.bfloat16)
    gain_grad = lax.optimization_barrier(jnp.sum(dnorm * attention * rscale, axis=(0, 1))).reshape(HEADS * HEAD)
    dattn = (dscaled * rscale - attention * (inner[:, :, None, None] * rscale ** 3 / (HEADS * HEAD))).astype(jnp.bfloat16)
    _, (query_grad, key_grad, value_grad) = lax.scan(block_backward, start, (query_blocks, key_blocks, value_blocks, decay_sum, dattn, prev_states), reverse=True)
    flat = (TOKEN_POSITIONS, HEADS * HEAD)
    return (query_grad.reshape(flat), key_grad.reshape(flat), value_grad.reshape(flat), gate_grad.reshape(flat), gain_grad)
```

```python
import functools

import jax
import jax.numpy as jnp
from jax import lax
from jax.experimental import pallas as pl
from jax.experimental.pallas import tpu as pltpu
from jax.sharding import PartitionSpec as P

HEAD = 128
BLOCK = 512
CHUNK = 128
CHUNKS = BLOCK // CHUNK
EPSILON = 1e-06
MESH = pl.DeviceIdType.MESH
F32, BF16 = jnp.float32, jnp.bfloat16

DECAY, GRAD, STATE_UP, STATE_DOWN, NORM, BACK_UP, BACK_DOWN, GAIN = range(8)


def dot(a, b, over_a, over_b):
    return lax.dot_general(
        a, b, (((over_a,), (over_b,)), ((), ())), preferred_element_type=F32
    )


def halves(x):
    high = x.astype(BF16)
    return high, (x - high.astype(F32)).astype(BF16)


def kernel(
    n, m, heads,
    ld_hbm, gain_hbm, k_hbm, v_hbm, q_hbm, gate_hbm, grad_hbm,
    dq_hbm, dk_hbm, dv_hbm, dgate_hbm, dgain_hbm,
    ld, gain, k, v, q, gate, grad,
    dq, dk, dv, dgate, dgain,
    ld_rows, tri, cum_col, cum_row, grow, shrink,
    table, probs, dscores, attention, dnorm, closed, dattn, q_high, q_low, dk_part, dv_part,
    decay_out, decay_in, up_out, up_in, down_out, down_in,
    norm_out, norm_in, coefs, columns,
    back_up_out, back_up_in, back_down_out, back_down_in, gain_out, gain_in,
    in_sem, out_sem, send_sem, recv_sem,
):
    me, mt = lax.axis_index("ctx"), lax.axis_index("tp")
    per_head = n // heads
    channels = heads * HEAD * m
    width = heads * HEAD
    grad_rows = BLOCK // m

    loads = [
        pltpu.make_async_copy(src, dst, in_sem.at[i])
        for i, (src, dst) in enumerate(
            ((ld_hbm, ld), (k_hbm, k), (v_hbm, v), (q_hbm, q), (gate_hbm, gate), (gain_hbm, gain))
        )
    ]
    for load in loads:
        load.start()
    own_grad = pltpu.make_async_copy(
        grad_hbm.at[:, pl.ds(pl.multiple_of(mt * width, width), width)],
        grad.at[pl.ds(pl.multiple_of(mt * grad_rows, grad_rows), grad_rows), :],
        in_sem.at[6],
    )
    own_grad.start()

    def to_ctx(i):
        return lax.rem(me + i, n)

    def to_tp(i):
        return lax.rem(mt + i, m)

    barrier = pltpu.get_barrier_semaphore()

    @pl.loop(1, n)
    def _(i):
        pl.semaphore_signal(barrier, inc=1, device_id={"ctx": to_ctx(i), "tp": mt}, device_id_type=MESH)

    @pl.loop(1, m)
    def _(i):
        pl.semaphore_signal(barrier, inc=1, device_id={"ctx": me, "tp": to_tp(i)}, device_id_type=MESH)

    def send(src, dst, which, peer):
        pltpu.make_async_remote_copy(
            src_ref=src,
            dst_ref=dst,
            send_sem=send_sem.at[which],
            recv_sem=recv_sem.at[which],
            device_id=peer,
            device_id_type=MESH,
        ).start()

    def scatter(out, into, which):
        into[me] = out[me]

        @pl.loop(1, n)
        def _(i):
            peer = to_ctx(i)
            send(out.at[peer], into.at[me], which, {"ctx": peer, "tp": mt})

    def arrived(into, which, count):
        some = into.at[pl.ds(0, count)]
        pltpu.make_async_copy(some, some, recv_sem.at[which]).wait()

    def sent(out, which, count):
        some = out.at[pl.ds(0, count)]
        pltpu.make_async_copy(some, some, send_sem.at[which]).wait()

    t = lax.broadcasted_iota(jnp.int32, (BLOCK, BLOCK), 0)
    u = lax.broadcasted_iota(jnp.int32, (BLOCK, BLOCK), 1)
    tri[...] = jnp.where(t >= u, 1.0, 0.0).astype(BF16)
    ld_rows[...] = jnp.zeros_like(ld_rows)
    coefs[...] = jnp.zeros_like(coefs)
    loads[0].wait()
    ld_rows[0:heads, :] = ld[...]
    whole = ld_rows[...]
    part0 = whole.astype(BF16)
    rest = whole - part0.astype(F32)
    part1 = rest.astype(BF16)
    part2 = (rest - part1.astype(F32)).astype(BF16)
    col = dot(tri[...], part0, 1, 1) + dot(tri[...], part1, 1, 1) + dot(tri[...], part2, 1, 1)
    cum_col[...] = col
    last = col[BLOCK - 1 : BLOCK, :]
    grow[...] = jnp.exp(col)
    shrink[...] = jnp.exp(last - col)
    for h in range(heads):
        decay_out[h] = jnp.broadcast_to(jnp.exp(last[:, h : h + 1]), (1, HEAD))

    pl.semaphore_wait(barrier, n - 1 + m - 1)

    decay_in[me] = decay_out[me // per_head]

    @pl.loop(1, n)
    def _(i):
        peer = to_ctx(i)
        send(decay_out.at[peer // per_head], decay_in.at[me], DECAY, {"ctx": peer, "tp": mt})

    @pl.loop(1, m)
    def _(i):
        peer = to_tp(i)
        send(
            grad_hbm.at[:, pl.ds(pl.multiple_of(peer * width, width), width)],
            grad.at[pl.ds(pl.multiple_of(mt * grad_rows, grad_rows), grad_rows), :],
            GRAD,
            {"ctx": me, "tp": peer},
        )

    def cols(h):
        return slice(h * HEAD, (h + 1) * HEAD)

    def rows(r):
        return slice(r * CHUNK, (r + 1) * CHUNK)

    def state(ref, h):
        return ref[h * per_head : (h + 1) * per_head].reshape(HEAD, HEAD)

    loads[1].wait()
    loads[2].wait()
    for h in range(heads):
        high, low = halves(k[:, cols(h)].astype(F32) * shrink[:, h : h + 1])
        addend = dot(high, v[:, cols(h)], 0, 0) + dot(low, v[:, cols(h)], 0, 0)
        up_out[h * per_head : (h + 1) * per_head] = addend.astype(BF16).reshape(per_head, HEAD // per_head, HEAD)
    scatter(up_out, up_in, STATE_UP)

    cum_row[...] = dot(part0, tri[...], 1, 1) + dot(part1, tri[...], 1, 1) + dot(part2, tri[...], 1, 1)
    loads[3].wait()

    def inside(h):
        for r in range(CHUNKS):
            w = (r + 1) * CHUNK
            scores = dot(q[rows(r), cols(h)], k[0:w, cols(h)], 1, 1)
            spread = cum_col[rows(r), h : h + 1] - cum_row[h : h + 1, 0:w]
            at = lax.broadcasted_iota(jnp.int32, (CHUNK, w), 0) + r * CHUNK
            weight = jnp.where(
                at >= lax.broadcasted_iota(jnp.int32, (CHUNK, w), 1),
                jnp.exp(jnp.minimum(spread, 0.0)),
                0.0,
            )
            table[h, rows(r), 0:w] = weight
            p = (scores * weight).astype(BF16)
            probs[h, rows(r), 0:w] = p
            attention[rows(r), cols(h)] = dot(p, v[0:w, cols(h)], 1, 0)
        high, low = halves(q[:, cols(h)].astype(F32) * grow[:, h : h + 1])
        q_high[:, cols(h)] = high
        q_low[:, cols(h)] = low

    for h in range(heads // 2):
        inside(h)

    arrived(decay_in, DECAY, n - 1)
    arrived(up_in, STATE_UP, n - 1)
    carried = jnp.zeros(up_in.shape[1:], F32)
    for j in range(n):
        down_out[j] = carried.astype(BF16)
        carried = carried * decay_in[j] + up_in[j].astype(F32)
    scatter(down_out, down_in, STATE_DOWN)

    for h in range(heads // 2, heads):
        inside(h)
    loads[4].wait()
    loads[5].wait()
    own_grad.wait()
    arriving = grad.at[pl.ds(0, (m - 1) * grad_rows), :]
    pltpu.make_async_copy(arriving, arriving, recv_sem.at[GRAD]).wait()
    for r in range(CHUNKS):
        for h in range(heads):
            opened = jax.nn.sigmoid(gate[rows(r), cols(h)].astype(F32))
            dnorm[rows(r), cols(h)] = grad[rows(r), cols(h)].astype(F32) * opened
            closed[rows(r), cols(h)] = 1.0 - opened

    arrived(down_in, STATE_DOWN, n - 1)
    ones = jnp.ones((16, HEAD), BF16)
    for r in range(CHUNKS):
        squares = jnp.zeros((CHUNK, HEAD), F32)
        inner = jnp.zeros((CHUNK, HEAD), F32)
        for h in range(heads):
            a = attention[rows(r), cols(h)] + grow[rows(r), h : h + 1] * dot(
                q[rows(r), cols(h)], state(down_in, h), 1, 0
            )
            attention[rows(r), cols(h)] = a
            squares = squares + a * a
            inner = inner + a * (dnorm[rows(r), cols(h)] * gain[h : h + 1, :])
        for place, total in ((r, squares), (CHUNKS + r, inner)):
            high, low = halves(total)
            line = dot(ones, high, 1, 1) + dot(ones, low, 1, 1)
            norm_out[place : place + 1, :] = line[0:1, :]

    norm_in[mt] = norm_out[...]

    @pl.loop(1, m)
    def _(i):
        send(norm_out, norm_in.at[mt], NORM, {"ctx": me, "tp": to_tp(i)})

    arrived(norm_in, NORM, m - 1)
    total = norm_in[0]
    for j in range(1, m):
        total = total + norm_in[j]
    rscale = lax.rsqrt(total[0:CHUNKS] / channels + EPSILON)
    coefs[0:CHUNKS, :] = rscale
    coefs[CHUNKS : 2 * CHUNKS, :] = total[CHUNKS : 2 * CHUNKS] * (rscale * rscale * rscale) / channels
    columns[...] = jnp.transpose(coefs[...])

    for r in range(CHUNKS):
        scale, pull = columns[:, r : r + 1], columns[:, CHUNKS + r : CHUNKS + r + 1]
        for h in range(heads):
            d = dnorm[rows(r), cols(h)] * gain[h : h + 1, :] * scale - attention[rows(r), cols(h)] * pull
            dattn[rows(r), cols(h)] = d.astype(BF16)
    for h in range(heads):
        addend = dot(q_high[:, cols(h)], dattn[:, cols(h)], 0, 0) + dot(q_low[:, cols(h)], dattn[:, cols(h)], 0, 0)
        back_up_out[h * per_head : (h + 1) * per_head] = addend.astype(BF16).reshape(per_head, HEAD // per_head, HEAD)
    scatter(back_up_out, back_up_in, BACK_UP)

    for h in range(heads):
        part = jnp.zeros((1, HEAD), F32)
        for r in range(CHUNKS):
            x = dnorm[rows(r), cols(h)] * attention[rows(r), cols(h)] * columns[:, r : r + 1]
            dgate[rows(r), cols(h)] = (x * gain[h : h + 1, :] * closed[rows(r), cols(h)]).astype(BF16)
            part = part + jnp.sum(x, axis=0, keepdims=True)
        gain_out[h : h + 1, :] = part
    stores = [pltpu.make_async_copy(dgate, dgate_hbm, out_sem.at[0])]
    stores[0].start()
    gain_in[me] = gain_out[...]

    @pl.loop(1, n)
    def _(i):
        send(gain_out, gain_in.at[me], GAIN, {"ctx": to_ctx(i), "tp": mt})

    def backward(h):
        for r in range(CHUNKS):
            w = (r + 1) * CHUNK
            d = dattn[rows(r), cols(h)]
            ds = (dot(d, v[0:w, cols(h)], 1, 1) * table[h, rows(r), 0:w]).astype(BF16)
            dscores[h, rows(r), 0:w] = ds
            inter = grow[rows(r), h : h + 1] * dot(d, state(down_in, h), 1, 1)
            dq[rows(r), cols(h)] = (dot(ds, k[0:w, cols(h)], 1, 0) + inter).astype(BF16)
        for c in range(CHUNKS):
            later = slice(c * CHUNK, BLOCK)
            dk_part[rows(c), cols(h)] = dot(dscores[h, later, rows(c)], q[later, cols(h)], 0, 0)
            dv_part[rows(c), cols(h)] = dot(probs[h, later, rows(c)], dattn[later, cols(h)], 0, 0)

    for h in range(heads // 2):
        backward(h)

    arrived(back_up_in, BACK_UP, n - 1)
    carried = jnp.zeros(back_up_in.shape[1:], F32)
    for j in reversed(range(n)):
        back_down_out[j] = carried.astype(BF16)
        carried = carried * decay_in[j] + back_up_in[j].astype(F32)
    scatter(back_down_out, back_down_in, BACK_DOWN)

    for h in range(heads // 2, heads):
        backward(h)
    stores.append(pltpu.make_async_copy(dq, dq_hbm, out_sem.at[1]))
    stores[-1].start()

    arrived(gain_in, GAIN, n - 1)
    total = gain_in[0]
    for j in range(1, n):
        total = total + gain_in[j]
    dgain[...] = total
    stores.append(pltpu.make_async_copy(dgain, dgain_hbm, out_sem.at[2]))
    stores[-1].start()

    arrived(back_down_in, BACK_DOWN, n - 1)
    for h in range(heads):
        back = state(back_down_in, h)
        fade = shrink[:, h : h + 1]
        dk[:, cols(h)] = (dk_part[:, cols(h)] + fade * dot(v[:, cols(h)], back, 1, 1)).astype(BF16)
        dv[:, cols(h)] = (dv_part[:, cols(h)] + fade * dot(k[:, cols(h)], back, 1, 0)).astype(BF16)
    for i, (src, dst) in enumerate(((dk, dk_hbm), (dv, dv_hbm))):
        stores.append(pltpu.make_async_copy(src, dst, out_sem.at[3 + i]))
        stores[-1].start()

    sent(decay_in, DECAY, n - 1)
    pltpu.make_async_copy(arriving, arriving, send_sem.at[GRAD]).wait()
    sent(up_out, STATE_UP, n - 1)
    sent(down_out, STATE_DOWN, n - 1)
    sent(norm_in, NORM, m - 1)
    sent(back_up_out, BACK_UP, n - 1)
    sent(back_down_out, BACK_DOWN, n - 1)
    sent(gain_in, GAIN, n - 1)
    for store in stores:
        store.wait()


def local(n, m, queries, keys, values, log_decay, gate, gain, grad_out):
    heads = queries.shape[1] // HEAD
    width = heads * HEAD
    assert queries.shape[0] == BLOCK and n % heads == 0
    piece = (heads * HEAD // n, HEAD)
    square = (BLOCK, width)
    pairs = (heads, BLOCK, BLOCK)
    vmem = pltpu.VMEM
    outs = pl.pallas_call(
        functools.partial(kernel, n, m, heads),
        out_shape=[jax.ShapeDtypeStruct(square, BF16)] * 4 + [jax.ShapeDtypeStruct((heads, HEAD), F32)],
        in_specs=[pl.BlockSpec(memory_space=pl.ANY)] * 7,
        out_specs=[pl.BlockSpec(memory_space=pl.ANY)] * 5,
        scratch_shapes=[
            vmem((heads, BLOCK), F32), vmem((heads, HEAD), F32),
            *[vmem(square, BF16)] * 5,
            *[vmem(square, BF16)] * 4, vmem((heads, HEAD), F32),
            vmem((16, BLOCK), F32), vmem((BLOCK, BLOCK), BF16),
            vmem((BLOCK, 16), F32), vmem((16, BLOCK), F32), vmem((BLOCK, 16), F32), vmem((BLOCK, 16), F32),
            vmem(pairs, F32), vmem(pairs, BF16), vmem(pairs, BF16),
            *[vmem(square, F32)] * 3, *[vmem(square, BF16)] * 3, *[vmem(square, F32)] * 2,
            vmem((heads, 1, HEAD), F32), vmem((n, 1, HEAD), F32),
            *[vmem((n, *piece), BF16)] * 4,
            vmem((2 * CHUNKS, CHUNK), F32), vmem((m, 2 * CHUNKS, CHUNK), F32),
            vmem((CHUNK, CHUNK), F32), vmem((CHUNK, CHUNK), F32),
            *[vmem((n, *piece), BF16)] * 4,
            vmem((heads, HEAD), F32), vmem((n, heads, HEAD), F32),
            pltpu.SemaphoreType.DMA((7,)), pltpu.SemaphoreType.DMA((5,)),
            pltpu.SemaphoreType.DMA((8,)), pltpu.SemaphoreType.DMA((8,)),
        ],
        compiler_params=pltpu.CompilerParams(
            collective_id=0, has_side_effects=True, vmem_limit_bytes=48 << 20
        ),
    )(log_decay, gain.reshape(heads, HEAD), keys, values, queries, gate, grad_out)
    dq, dk, dv, dgate, dgain = outs
    return dq, dk, dv, dgate, dgain.reshape(width)


def solution(mesh):
    return jax.shard_map(
        functools.partial(local, mesh.shape["ctx"], mesh.shape["tp"]),
        mesh=mesh,
        in_specs=(
            P("ctx", "tp"),
            P("ctx", "tp"),
            P("ctx", "tp"),
            P("tp", "ctx"),
            P("ctx", "tp"),
            P("tp"),
            P(("ctx", "tp"), None),
        ),
        out_specs=(P("ctx", "tp"), P("ctx", "tp"), P("ctx", "tp"), P("ctx", "tp"), P("tp")),
        check_vma=False,
    )
```

```python
import functools

import jax
import jax.numpy as jnp
from jax import lax
from jax.experimental import pallas as pl
from jax.experimental.pallas import tpu as pltpu
from jax.sharding import PartitionSpec as P

HEAD = 128
BLOCK = 512
CHUNK = 128
CHUNKS = BLOCK // CHUNK
EPSILON = 1e-06
MESH = pl.DeviceIdType.MESH
F32, BF16 = jnp.float32, jnp.bfloat16

DECAY_PAIR, DECAY, GRAD, NORM, GAIN_PAIR, GAIN, FORWARD, BACKWARD = 0, 1, 2, 3, 4, 5, 6, 11
URGENT, REST, UP, DOWN, WHOLE = range(5)
SEMAPHORES = 16


def dot(a, b, over_a, over_b):
    return lax.dot_general(
        a, b, (((over_a,), (over_b,)), ((), ())), preferred_element_type=F32
    )


def halves(x):
    high = x.astype(BF16)
    return high, (x - high.astype(F32)).astype(BF16)


def far_first(count):
    return sorted(range(count), key=lambda i: -min(i, count - i))


def kernel(
    n, m, heads,
    ld_hbm, gain_hbm, k_hbm, v_hbm, q_hbm, gate_hbm, grad_hbm,
    dq, dk, dv, dgate, dgain,
    ld, gain, k, v, q, gate, grad,
    ld_rows, tri, cum_col, cum_row, grow, shrink,
    table, probs, dscores, attention, dnorm, closed, dattn, q_high, q_low, dk_part, dv_part,
    decay_own, decay_pair, decay_out, decay_in,
    norm_out, norm_in, coefs, columns, gain_own, gain_pair, gain_in,
    fore_own, fore_out, fore_pair, fore_up_out, fore_up_in, fore_down, fore_whole, fore_state,
    back_own, back_out, back_pair, back_up_out, back_up_in, back_down, back_whole,
    in_sem, send_sem, recv_sem,
):
    me, mt = lax.axis_index("ctx"), lax.axis_index("tp")
    core, chip = lax.rem(me, 2), me // 2
    chips, deep = n // 2, n // 4
    per_head = n // heads
    channels = heads * HEAD * m
    width = heads * HEAD
    grad_rows = BLOCK // m
    half = pl.ds(core * chips, chips)
    other_half = pl.ds((1 - core) * chips, chips)

    loads = [
        pltpu.make_async_copy(src, dst, in_sem.at[i])
        for i, (src, dst) in enumerate(
            ((ld_hbm, ld), (k_hbm, k), (v_hbm, v), (q_hbm, q), (gate_hbm, gate), (gain_hbm, gain))
        )
    ]
    for load in loads:
        load.start()

    peers = [
        lax.rem(chip // deep + y, 2) * deep + lax.rem(chip + z, deep)
        for z in far_first(deep)
        for y in (1, 0)
        if (y, z) != (0, 0)
    ]
    tp_peers = [
        lax.rem(mt // 2 + x, m // 2) * 2 + lax.rem(mt + y, 2)
        for y in (1, 0)
        for x in far_first(m // 2)
        if (y, x) != (0, 0)
    ]

    def on_chip(p):
        return {"ctx": 2 * p + core, "tp": mt}

    def on_tp(p):
        return {"ctx": me, "tp": p}

    sibling = {"ctx": 2 * chip + 1 - core, "tp": mt}

    barrier = pltpu.get_barrier_semaphore()
    greeted = [on_chip(p) for p in peers] + [on_tp(p) for p in tp_peers] + [sibling]
    for device in greeted:
        pl.semaphore_signal(barrier, inc=1, device_id=device, device_id_type=MESH)

    def send(src, dst, which, device):
        pltpu.make_async_remote_copy(
            src_ref=src,
            dst_ref=dst,
            send_sem=send_sem.at[which],
            recv_sem=recv_sem.at[which],
            device_id=device,
            device_id_type=MESH,
        ).start()

    def arrived(some, which):
        pltpu.make_async_copy(some, some, recv_sem.at[which]).wait()

    def sent(some, which):
        pltpu.make_async_copy(some, some, send_sem.at[which]).wait()

    def cols(h):
        return slice(h * HEAD, (h + 1) * HEAD)

    def rows(r):
        return slice(r * CHUNK, (r + 1) * CHUNK)

    def pieces(h):
        return slice(h * per_head, (h + 1) * per_head)

    def state(ref, h):
        return ref[pieces(h)].reshape(HEAD, HEAD)

    t = lax.broadcasted_iota(jnp.int32, (BLOCK, BLOCK), 0)
    u = lax.broadcasted_iota(jnp.int32, (BLOCK, BLOCK), 1)
    tri[...] = jnp.where(t >= u, 1.0, 0.0).astype(BF16)
    ld_rows[...] = jnp.zeros_like(ld_rows)
    coefs[...] = jnp.zeros_like(coefs)
    loads[0].wait()
    ld_rows[0:heads, :] = ld[...]
    whole = ld_rows[...]
    part0 = whole.astype(BF16)
    rest = whole - part0.astype(F32)
    part1 = rest.astype(BF16)
    part2 = (rest - part1.astype(F32)).astype(BF16)
    col = dot(tri[...], part0, 1, 1) + dot(tri[...], part1, 1, 1) + dot(tri[...], part2, 1, 1)
    cum_col[...] = col
    last = col[BLOCK - 1 : BLOCK, :]
    grow[...] = jnp.exp(col)
    shrink[...] = jnp.exp(last - col)
    for h in range(heads):
        decay_own[h] = jnp.broadcast_to(jnp.exp(last[:, h : h + 1]), (1, HEAD))

    pl.semaphore_wait(barrier, len(greeted))
    send(decay_own, decay_pair, DECAY_PAIR, sibling)

    def share(h, addend, own, out):
        addend = addend.reshape(per_head, HEAD // per_head, HEAD)
        own[pieces(h)] = addend
        out[pieces(h)] = addend.astype(BF16)

    def swap(out, pair, first):
        send(out.at[other_half], pair.at[other_half], first + URGENT, sibling)
        send(out.at[half], pair.at[half], first + REST, sibling)

    def join(own, pair, up_out, up_in, leads, first):
        arrived(pair.at[half], first + URGENT)
        for g in range(heads // 2):
            h = core * (heads // 2) + g
            here = pl.ds(core * chips + g * per_head, per_head)
            by_own = leads * decay_pair[h] + (1.0 - leads)
            by_pair = leads + (1.0 - leads) * decay_own[h]
            up_out[pieces(g)] = (own[here] * by_own + pair[here].astype(F32) * by_pair).astype(BF16)
        for p in peers:
            send(up_out.at[p], up_in.at[chip], first + UP, on_chip(p))
        up_in[chip] = up_out[chip]

    def scan(up_in, down, whole, order, first):
        arrived(up_in.at[pl.ds(0, chips - 1)], first + UP)
        carried = jnp.zeros(up_in.shape[1:], F32)
        for j in order:
            down[j] = carried.astype(BF16)
            carried = carried * decay_in[j] + up_in[j].astype(F32)
        for p in peers:
            send(down.at[p], whole.at[core * chips + chip], first + DOWN, on_chip(p))
        whole[core * chips + chip] = down[chip]

    def settle(whole, pair, first):
        arrived(whole.at[pl.ds(0, chips - 1)], first + DOWN)
        send(whole.at[half], whole.at[half], first + WHOLE, sibling)
        arrived(pair.at[other_half], first + REST)
        arrived(whole.at[other_half], first + WHOLE)

    def entering(whole, pair, leads, h):
        by_chip = leads + (1.0 - leads) * decay_pair[h]
        held = whole[pieces(h)].astype(F32) * by_chip + pair[pieces(h)].astype(F32) * (1.0 - leads)
        return held.astype(BF16)

    fore_leads = (1 - core).astype(F32)
    back_leads = core.astype(F32)

    loads[1].wait()
    loads[2].wait()
    for h in range(heads):
        high, low = halves(k[:, cols(h)].astype(F32) * shrink[:, h : h + 1])
        share(h, dot(high, v[:, cols(h)], 0, 0) + dot(low, v[:, cols(h)], 0, 0), fore_own, fore_out)
    swap(fore_out, fore_pair, FORWARD)

    arrived(decay_pair, DECAY_PAIR)
    decay_out[...] = decay_own[...] * decay_pair[...]
    for p in peers:
        send(decay_out.at[(core * chips + p) // per_head], decay_in.at[chip], DECAY, on_chip(p))
    decay_in[chip] = decay_out[(core * chips + chip) // per_head]
    join(fore_own, fore_pair, fore_up_out, fore_up_in, fore_leads, FORWARD)

    def grad_part(p):
        return grad_hbm.at[:, pl.ds(pl.multiple_of(p * width, width), width)]

    grad_place = grad.at[pl.ds(pl.multiple_of(mt * grad_rows, grad_rows), grad_rows), :]
    own_grad = pltpu.make_async_copy(grad_part(mt), grad_place, in_sem.at[6])
    own_grad.start()
    for p in tp_peers:
        send(grad_part(p), grad_place, GRAD, on_tp(p))

    cum_row[...] = dot(part0, tri[...], 1, 1) + dot(part1, tri[...], 1, 1) + dot(part2, tri[...], 1, 1)
    loads[3].wait()

    def inside(h):
        for r in range(CHUNKS):
            w = (r + 1) * CHUNK
            scores = dot(q[rows(r), cols(h)], k[0:w, cols(h)], 1, 1)
            spread = cum_col[rows(r), h : h + 1] - cum_row[h : h + 1, 0:w]
            at = lax.broadcasted_iota(jnp.int32, (CHUNK, w), 0) + r * CHUNK
            weight = jnp.where(
                at >= lax.broadcasted_iota(jnp.int32, (CHUNK, w), 1),
                jnp.exp(jnp.minimum(spread, 0.0)),
                0.0,
            )
            table[h, rows(r), 0:w] = weight
            p = (scores * weight).astype(BF16)
            probs[h, rows(r), 0:w] = p
            attention[rows(r), cols(h)] = dot(p, v[0:w, cols(h)], 1, 0)
        high, low = halves(q[:, cols(h)].astype(F32) * grow[:, h : h + 1])
        q_high[cols(h), :] = jnp.transpose(high)
        q_low[cols(h), :] = jnp.transpose(low)

    for h in range(heads // 2):
        inside(h)

    arrived(decay_in.at[pl.ds(0, chips - 1)], DECAY)
    scan(fore_up_in, fore_down, fore_whole, range(chips), FORWARD)

    for h in range(heads // 2, heads):
        inside(h)
    loads[4].wait()
    loads[5].wait()
    own_grad.wait()
    arriving = grad.at[pl.ds(0, (m - 1) * grad_rows), :]
    arrived(arriving, GRAD)
    for r in range(CHUNKS):
        for h in range(heads):
            opened = jax.nn.sigmoid(gate[rows(r), cols(h)].astype(F32))
            dnorm[rows(r), cols(h)] = grad[rows(r), cols(h)].astype(F32) * opened
            closed[rows(r), cols(h)] = 1.0 - opened

    settle(fore_whole, fore_pair, FORWARD)
    for h in range(heads):
        fore_state[pieces(h)] = entering(fore_whole, fore_pair, fore_leads, h)
    ones = jnp.ones((16, HEAD), BF16)
    for r in range(CHUNKS):
        squares = jnp.zeros((CHUNK, HEAD), F32)
        inner = jnp.zeros((CHUNK, HEAD), F32)
        for h in range(heads):
            a = attention[rows(r), cols(h)] + grow[rows(r), h : h + 1] * dot(
                q[rows(r), cols(h)], state(fore_state, h), 1, 0
            )
            attention[rows(r), cols(h)] = a
            squares = squares + a * a
            inner = inner + a * (dnorm[rows(r), cols(h)] * gain[h : h + 1, :])
        for place, total in ((r, squares), (CHUNKS + r, inner)):
            high, low = halves(total)
            line = dot(ones, high, 1, 1) + dot(ones, low, 1, 1)
            norm_out[place : place + 1, :] = line[0:1, :]
    for p in tp_peers:
        send(norm_out, norm_in.at[mt], NORM, on_tp(p))
    norm_in[mt] = norm_out[...]
    arrived(norm_in.at[pl.ds(0, m - 1)], NORM)
    total = norm_in[0]
    for j in range(1, m):
        total = total + norm_in[j]
    rscale = lax.rsqrt(total[0:CHUNKS] / channels + EPSILON)
    coefs[0:CHUNKS, :] = rscale
    coefs[CHUNKS : 2 * CHUNKS, :] = total[CHUNKS : 2 * CHUNKS] * (rscale * rscale * rscale) / channels
    columns[...] = jnp.transpose(coefs[...])

    for r in range(CHUNKS):
        scale, pull = columns[:, r : r + 1], columns[:, CHUNKS + r : CHUNKS + r + 1]
        for h in range(heads):
            d = dnorm[rows(r), cols(h)] * gain[h : h + 1, :] * scale - attention[rows(r), cols(h)] * pull
            dattn[rows(r), cols(h)] = d.astype(BF16)
    for h in range(heads):
        share(h, dot(q_high[cols(h), :], dattn[:, cols(h)], 1, 0) + dot(q_low[cols(h), :], dattn[:, cols(h)], 1, 0), back_own, back_out)
    swap(back_out, back_pair, BACKWARD)

    for h in range(heads):
        part = jnp.zeros((1, HEAD), F32)
        for r in range(CHUNKS):
            x = dnorm[rows(r), cols(h)] * attention[rows(r), cols(h)] * columns[:, r : r + 1]
            dgate[rows(r), cols(h)] = (x * gain[h : h + 1, :] * closed[rows(r), cols(h)]).astype(BF16)
            part = part + jnp.sum(x, axis=0, keepdims=True)
        gain_own[h : h + 1, :] = part
    send(gain_own, gain_pair, GAIN_PAIR, sibling)
    join(back_own, back_pair, back_up_out, back_up_in, back_leads, BACKWARD)

    def backward(h):
        for r in range(CHUNKS):
            w = (r + 1) * CHUNK
            d = dattn[rows(r), cols(h)]
            ds = (dot(d, v[0:w, cols(h)], 1, 1) * table[h, rows(r), 0:w]).astype(BF16)
            dscores[h, rows(r), 0:w] = ds
            inter = grow[rows(r), h : h + 1] * dot(d, state(fore_state, h), 1, 1)
            dq[rows(r), cols(h)] = (dot(ds, k[0:w, cols(h)], 1, 0) + inter).astype(BF16)
        for c in range(CHUNKS):
            later = slice(c * CHUNK, BLOCK)
            dk_part[rows(c), cols(h)] = dot(dscores[h, later, rows(c)], q[later, cols(h)], 0, 0)
            dv_part[rows(c), cols(h)] = dot(probs[h, later, rows(c)], dattn[later, cols(h)], 0, 0)

    backward(0)
    arrived(gain_pair, GAIN_PAIR)
    gain_in[chip] = gain_own[...] + gain_pair[...]
    for p in peers:
        send(gain_in.at[chip], gain_in.at[chip], GAIN, on_chip(p))
    for h in range(1, heads // 2):
        backward(h)

    scan(back_up_in, back_down, back_whole, reversed(range(chips)), BACKWARD)

    for h in range(heads // 2, heads):
        backward(h)

    arrived(gain_in.at[pl.ds(0, chips - 1)], GAIN)
    total = gain_in[0]
    for j in range(1, chips):
        total = total + gain_in[j]
    dgain[...] = total

    settle(back_whole, back_pair, BACKWARD)
    for h in range(heads):
        back = entering(back_whole, back_pair, back_leads, h).reshape(HEAD, HEAD)
        fade = shrink[:, h : h + 1]
        dk[:, cols(h)] = (dk_part[:, cols(h)] + fade * dot(v[:, cols(h)], back, 1, 1)).astype(BF16)
        dv[:, cols(h)] = (dv_part[:, cols(h)] + fade * dot(k[:, cols(h)], back, 1, 0)).astype(BF16)

    sent(decay_own, DECAY_PAIR)
    sent(decay_in.at[pl.ds(0, chips - 1)], DECAY)
    sent(arriving, GRAD)
    sent(norm_in.at[pl.ds(0, m - 1)], NORM)
    sent(gain_own, GAIN_PAIR)
    sent(gain_in.at[pl.ds(0, chips - 1)], GAIN)
    for first, up_out in ((FORWARD, fore_up_out), (BACKWARD, back_up_out)):
        one_less = up_out.at[pl.ds(0, chips - 1)]
        for which, some in ((URGENT, up_out), (REST, up_out), (UP, one_less), (DOWN, one_less), (WHOLE, up_out)):
            sent(some, first + which)


def put(*refs):
    sem, half = refs[-1], len(refs) // 2
    copies = [pltpu.make_async_copy(refs[i], refs[half + i], sem.at[i]) for i in range(half)]
    for copy in copies:
        copy.start()
    for copy in copies:
        copy.wait()


def local(n, m, queries, keys, values, log_decay, gate, gain, grad_out):
    heads = queries.shape[1] // HEAD
    width = heads * HEAD
    assert queries.shape[0] == BLOCK and n % heads == 0
    piece = (heads * HEAD // n, HEAD)
    square = (BLOCK, width)
    pairs = (heads, BLOCK, BLOCK)
    vmem = pltpu.VMEM
    sweep = [
        vmem((n, *piece), F32), *[vmem((n, *piece), BF16)] * 2,
        *[vmem((n // 2, *piece), BF16)] * 3, vmem((n, *piece), BF16),
    ]
    outs = pl.pallas_call(
        functools.partial(kernel, n, m, heads),
        out_shape=[jax.ShapeDtypeStruct(square, BF16)] * 4 + [jax.ShapeDtypeStruct((heads, HEAD), F32)],
        in_specs=[pl.BlockSpec(memory_space=pltpu.HBM)] * 7,
        out_specs=[pl.BlockSpec(memory_space=pltpu.VMEM)] * 5,
        scratch_shapes=[
            vmem((heads, BLOCK), F32), vmem((heads, HEAD), F32),
            *[vmem(square, BF16)] * 5,
            vmem((16, BLOCK), F32), vmem((BLOCK, BLOCK), BF16),
            vmem((BLOCK, 16), F32), vmem((16, BLOCK), F32), vmem((BLOCK, 16), F32), vmem((BLOCK, 16), F32),
            vmem(pairs, F32), vmem(pairs, BF16), vmem(pairs, BF16),
            *[vmem(square, F32)] * 3, vmem(square, BF16), *[vmem((width, BLOCK), BF16)] * 2, *[vmem(square, F32)] * 2,
            *[vmem((heads, 1, HEAD), F32)] * 3, vmem((n // 2, 1, HEAD), F32),
            vmem((2 * CHUNKS, CHUNK), F32), vmem((m, 2 * CHUNKS, CHUNK), F32),
            vmem((CHUNK, CHUNK), F32), vmem((CHUNK, CHUNK), F32),
            *[vmem((heads, HEAD), F32)] * 2, vmem((n // 2, heads, HEAD), F32),
            *sweep, vmem((n, *piece), BF16),
            *sweep,
            pltpu.SemaphoreType.DMA((7,)),
            pltpu.SemaphoreType.DMA((SEMAPHORES,)), pltpu.SemaphoreType.DMA((SEMAPHORES,)),
        ],
        compiler_params=pltpu.CompilerParams(
            collective_id=0, has_side_effects=True, vmem_limit_bytes=48 << 20
        ),
    )(*[pltpu.with_memory_space_constraint(x, pltpu.HBM) for x in (log_decay, gain.reshape(heads, HEAD), keys, values, queries, gate, grad_out)])
    dq, dk, dv, dgate, dgain = pl.pallas_call(
        put,
        out_shape=[jax.ShapeDtypeStruct(x.shape, x.dtype) for x in outs],
        in_specs=[pl.BlockSpec(memory_space=pl.ANY)] * len(outs),
        out_specs=[pl.BlockSpec(memory_space=pltpu.HBM)] * len(outs),
        scratch_shapes=[pltpu.SemaphoreType.DMA((len(outs),))],
    )(*[pltpu.with_memory_space_constraint(x, pltpu.VMEM) for x in outs])
    return dq, dk, dv, dgate, dgain.reshape(width)


def solution(mesh):
    return jax.shard_map(
        functools.partial(local, mesh.shape["ctx"], mesh.shape["tp"]),
        mesh=mesh,
        in_specs=(
            P("ctx", "tp"),
            P("ctx", "tp"),
            P("ctx", "tp"),
            P("tp", "ctx"),
            P("ctx", "tp"),
            P("tp"),
            P(("ctx", "tp"), None),
        ),
        out_specs=(P("ctx", "tp"), P("ctx", "tp"), P("ctx", "tp"), P("ctx", "tp"), P("tp")),
        check_vma=False,
    )
```

```python
import functools

import jax
import jax.numpy as jnp
from jax import lax
from jax.experimental import pallas as pl
from jax.experimental.pallas import tpu as pltpu
from jax.sharding import PartitionSpec as P

HEAD = 128
BLOCK = 512
CHUNK = 128
CHUNKS = BLOCK // CHUNK
EPSILON = 1e-06
MESH = pl.DeviceIdType.MESH
F32, BF16 = jnp.float32, jnp.bfloat16

DECAY_PAIR, DECAY, GRAD, NORM, GAIN_PAIR, GAIN, FORWARD, BACKWARD = 0, 1, 2, 3, 4, 5, 6, 11
URGENT, REST, UP, DOWN, WHOLE = range(5)
SEMAPHORES = 16


def dot(a, b, over_a, over_b):
    return lax.dot_general(
        a, b, (((over_a,), (over_b,)), ((), ())), preferred_element_type=F32
    )


def halves(x):
    high = x.astype(BF16)
    return high, (x - high.astype(F32)).astype(BF16)


def far_first(count):
    return sorted(range(count), key=lambda i: -min(i, count - i))


def kernel(
    n, m, heads,
    ld_hbm, gain_hbm, k_hbm, v_hbm, q_hbm, gate_hbm, grad_hbm,
    dq, dgate, dgain, k, v, shrink, back_state, dk_part, dv_part,
    ld, gain, q, gate, grad,
    ld_rows, tri, cum_col, cum_row, grow,
    table, probs, dscores, attention, dnorm, closed, dattn, q_high, q_low,
    decay_own, decay_pair, decay_out, decay_in,
    norm_out, norm_in, coefs, columns, gain_own, gain_pair, gain_in,
    fore_own, fore_out, fore_pair, fore_up_out, fore_up_in, fore_down, fore_whole, fore_state,
    back_own, back_out, back_pair, back_up_out, back_up_in, back_down, back_whole,
    in_sem, send_sem, recv_sem,
):
    me, mt = lax.axis_index("ctx"), lax.axis_index("tp")
    core, chip = lax.rem(me, 2), me // 2
    chips, deep = n // 2, n // 4
    per_head = n // heads
    channels = heads * HEAD * m
    width = heads * HEAD
    grad_rows = BLOCK // m
    half = pl.ds(core * chips, chips)
    other_half = pl.ds((1 - core) * chips, chips)

    loads = [
        pltpu.make_async_copy(src, dst, in_sem.at[i])
        for i, (src, dst) in enumerate(
            ((ld_hbm, ld), (k_hbm, k), (v_hbm, v), (q_hbm, q), (gate_hbm, gate), (gain_hbm, gain))
        )
    ]
    for load in loads:
        load.start()

    peers = [
        lax.rem(chip // deep + y, 2) * deep + lax.rem(chip + z, deep)
        for z in far_first(deep)
        for y in (1, 0)
        if (y, z) != (0, 0)
    ]
    tp_peers = [
        lax.rem(mt // 2 + x, m // 2) * 2 + lax.rem(mt + y, 2)
        for y in (1, 0)
        for x in far_first(m // 2)
        if (y, x) != (0, 0)
    ]

    def on_chip(p):
        return {"ctx": 2 * p + core, "tp": mt}

    def on_tp(p):
        return {"ctx": me, "tp": p}

    sibling = {"ctx": 2 * chip + 1 - core, "tp": mt}

    barrier = pltpu.get_barrier_semaphore()
    greeted = [on_chip(p) for p in peers] + [on_tp(p) for p in tp_peers] + [sibling]
    for device in greeted:
        pl.semaphore_signal(barrier, inc=1, device_id=device, device_id_type=MESH)

    def send(src, dst, which, device):
        pltpu.make_async_remote_copy(
            src_ref=src,
            dst_ref=dst,
            send_sem=send_sem.at[which],
            recv_sem=recv_sem.at[which],
            device_id=device,
            device_id_type=MESH,
        ).start()

    def arrived(some, which):
        pltpu.make_async_copy(some, some, recv_sem.at[which]).wait()

    def sent(some, which):
        pltpu.make_async_copy(some, some, send_sem.at[which]).wait()

    def cols(h):
        return slice(h * HEAD, (h + 1) * HEAD)

    def rows(r):
        return slice(r * CHUNK, (r + 1) * CHUNK)

    def pieces(h):
        return slice(h * per_head, (h + 1) * per_head)

    def state(ref, h):
        return ref[pieces(h)].reshape(HEAD, HEAD)

    t = lax.broadcasted_iota(jnp.int32, (BLOCK, BLOCK), 0)
    u = lax.broadcasted_iota(jnp.int32, (BLOCK, BLOCK), 1)
    tri[...] = jnp.where(t >= u, 1.0, 0.0).astype(BF16)
    ld_rows[...] = jnp.zeros_like(ld_rows)
    coefs[...] = jnp.zeros_like(coefs)
    loads[0].wait()
    ld_rows[0:heads, :] = ld[...]
    whole = ld_rows[...]
    part0 = whole.astype(BF16)
    rest = whole - part0.astype(F32)
    part1 = rest.astype(BF16)
    part2 = (rest - part1.astype(F32)).astype(BF16)
    col = dot(tri[...], part0, 1, 1) + dot(tri[...], part1, 1, 1) + dot(tri[...], part2, 1, 1)
    cum_col[...] = col
    last = col[BLOCK - 1 : BLOCK, :]
    grow[...] = jnp.exp(col)
    shrink[...] = jnp.exp(last - col)
    for h in range(heads):
        decay_own[h] = jnp.broadcast_to(jnp.exp(last[:, h : h + 1]), (1, HEAD))

    def share(h, addend, own, out):
        addend = addend.reshape(per_head, HEAD // per_head, HEAD)
        own[pieces(h)] = addend
        out[pieces(h)] = addend.astype(BF16)

    def swap(out, pair, first):
        send(out.at[other_half], pair.at[other_half], first + URGENT, sibling)
        send(out.at[half], pair.at[half], first + REST, sibling)

    def join(own, pair, up_out, up_in, leads, first):
        arrived(pair.at[half], first + URGENT)
        for g in range(heads // 2):
            h = core * (heads // 2) + g
            here = pl.ds(core * chips + g * per_head, per_head)
            by_own = leads * decay_pair[h] + (1.0 - leads)
            by_pair = leads + (1.0 - leads) * decay_own[h]
            up_out[pieces(g)] = (own[here] * by_own + pair[here].astype(F32) * by_pair).astype(BF16)
        for p in peers:
            send(up_out.at[p], up_in.at[chip], first + UP, on_chip(p))
        up_in[chip] = up_out[chip]

    def scan(up_in, down, whole, order, first):
        arrived(up_in.at[pl.ds(0, chips - 1)], first + UP)
        carried = jnp.zeros(up_in.shape[1:], F32)
        for j in order:
            down[j] = carried.astype(BF16)
            carried = carried * decay_in[j] + up_in[j].astype(F32)
        for p in peers:
            send(down.at[p], whole.at[core * chips + chip], first + DOWN, on_chip(p))
        whole[core * chips + chip] = down[chip]

    def settle(whole, pair, first):
        arrived(whole.at[pl.ds(0, chips - 1)], first + DOWN)
        send(whole.at[half], whole.at[half], first + WHOLE, sibling)
        arrived(pair.at[other_half], first + REST)
        arrived(whole.at[other_half], first + WHOLE)

    def entering(whole, pair, leads, h):
        by_chip = leads + (1.0 - leads) * decay_pair[h]
        held = whole[pieces(h)].astype(F32) * by_chip + pair[pieces(h)].astype(F32) * (1.0 - leads)
        return held.astype(BF16)

    fore_leads = (1 - core).astype(F32)
    back_leads = core.astype(F32)

    loads[1].wait()
    loads[2].wait()
    for h in range(heads):
        high, low = halves(k[:, cols(h)].astype(F32) * shrink[:, h : h + 1])
        share(h, dot(high, v[:, cols(h)], 0, 0) + dot(low, v[:, cols(h)], 0, 0), fore_own, fore_out)
    pl.semaphore_wait(barrier, len(greeted))
    send(decay_own, decay_pair, DECAY_PAIR, sibling)
    swap(fore_out, fore_pair, FORWARD)

    def grad_part(p):
        return grad_hbm.at[:, pl.ds(pl.multiple_of(p * width, width), width)]

    grad_place = grad.at[pl.ds(pl.multiple_of(mt * grad_rows, grad_rows), grad_rows), :]
    own_grad = pltpu.make_async_copy(grad_part(mt), grad_place, in_sem.at[6])
    own_grad.start()
    for p in tp_peers:
        send(grad_part(p), grad_place, GRAD, on_tp(p))

    arrived(decay_pair, DECAY_PAIR)
    decay_out[...] = decay_own[...] * decay_pair[...]
    for p in peers:
        send(decay_out.at[(core * chips + p) // per_head], decay_in.at[chip], DECAY, on_chip(p))
    decay_in[chip] = decay_out[(core * chips + chip) // per_head]
    join(fore_own, fore_pair, fore_up_out, fore_up_in, fore_leads, FORWARD)

    cum_row[...] = dot(part0, tri[...], 1, 1) + dot(part1, tri[...], 1, 1) + dot(part2, tri[...], 1, 1)
    loads[3].wait()

    def inside(h):
        for r in range(CHUNKS):
            w = (r + 1) * CHUNK
            scores = dot(q[rows(r), cols(h)], k[0:w, cols(h)], 1, 1)
            spread = cum_col[rows(r), h : h + 1] - cum_row[h : h + 1, 0:w]
            at = lax.broadcasted_iota(jnp.int32, (CHUNK, w), 0) + r * CHUNK
            weight = jnp.where(
                at >= lax.broadcasted_iota(jnp.int32, (CHUNK, w), 1),
                jnp.exp(jnp.minimum(spread, 0.0)),
                0.0,
            )
            table[h, rows(r), 0:w] = weight
            p = (scores * weight).astype(BF16)
            probs[h, rows(r), 0:w] = p
            attention[rows(r), cols(h)] = dot(p, v[0:w, cols(h)], 1, 0)
        high, low = halves(q[:, cols(h)].astype(F32) * grow[:, h : h + 1])
        q_high[cols(h), :] = jnp.transpose(high)
        q_low[cols(h), :] = jnp.transpose(low)

    for h in range(heads // 2):
        inside(h)

    arrived(decay_in.at[pl.ds(0, chips - 1)], DECAY)
    scan(fore_up_in, fore_down, fore_whole, range(chips), FORWARD)

    for h in range(heads // 2, heads):
        inside(h)
    loads[4].wait()
    loads[5].wait()
    own_grad.wait()
    arriving = grad.at[pl.ds(0, (m - 1) * grad_rows), :]
    arrived(arriving, GRAD)
    for r in range(CHUNKS):
        for h in range(heads):
            opened = jax.nn.sigmoid(gate[rows(r), cols(h)].astype(F32))
            dnorm[rows(r), cols(h)] = grad[rows(r), cols(h)].astype(F32) * opened
            closed[rows(r), cols(h)] = 1.0 - opened

    settle(fore_whole, fore_pair, FORWARD)
    for h in range(heads):
        fore_state[pieces(h)] = entering(fore_whole, fore_pair, fore_leads, h)
    ones = jnp.ones((16, HEAD), BF16)
    for r in range(CHUNKS):
        squares = jnp.zeros((CHUNK, HEAD), F32)
        inner = jnp.zeros((CHUNK, HEAD), F32)
        for h in range(heads):
            a = attention[rows(r), cols(h)] + grow[rows(r), h : h + 1] * dot(
                q[rows(r), cols(h)], state(fore_state, h), 1, 0
            )
            attention[rows(r), cols(h)] = a
            squares = squares + a * a
            inner = inner + a * (dnorm[rows(r), cols(h)] * gain[h : h + 1, :])
        for place, total in ((r, squares), (CHUNKS + r, inner)):
            high, low = halves(total)
            line = dot(ones, high, 1, 1) + dot(ones, low, 1, 1)
            norm_out[place : place + 1, :] = line[0:1, :]
    for p in tp_peers:
        send(norm_out, norm_in.at[mt], NORM, on_tp(p))
    norm_in[mt] = norm_out[...]
    arrived(norm_in.at[pl.ds(0, m - 1)], NORM)
    total = norm_in[0]
    for j in range(1, m):
        total = total + norm_in[j]
    rscale = lax.rsqrt(total[0:CHUNKS] / channels + EPSILON)
    coefs[0:CHUNKS, :] = rscale
    coefs[CHUNKS : 2 * CHUNKS, :] = total[CHUNKS : 2 * CHUNKS] * (rscale * rscale * rscale) / channels
    columns[...] = jnp.transpose(coefs[...])

    for r in range(CHUNKS):
        scale, pull = columns[:, r : r + 1], columns[:, CHUNKS + r : CHUNKS + r + 1]
        for h in range(heads):
            d = dnorm[rows(r), cols(h)] * gain[h : h + 1, :] * scale - attention[rows(r), cols(h)] * pull
            dattn[rows(r), cols(h)] = d.astype(BF16)
    for h in range(heads):
        share(h, dot(q_high[cols(h), :], dattn[:, cols(h)], 1, 0) + dot(q_low[cols(h), :], dattn[:, cols(h)], 1, 0), back_own, back_out)
    swap(back_out, back_pair, BACKWARD)

    for h in range(heads):
        part = jnp.zeros((1, HEAD), F32)
        for r in range(CHUNKS):
            x = dnorm[rows(r), cols(h)] * attention[rows(r), cols(h)] * columns[:, r : r + 1]
            dgate[rows(r), cols(h)] = (x * gain[h : h + 1, :] * closed[rows(r), cols(h)]).astype(BF16)
            part = part + jnp.sum(x, axis=0, keepdims=True)
        gain_own[h : h + 1, :] = part
    send(gain_own, gain_pair, GAIN_PAIR, sibling)
    join(back_own, back_pair, back_up_out, back_up_in, back_leads, BACKWARD)

    def backward(h):
        for r in range(CHUNKS):
            w = (r + 1) * CHUNK
            d = dattn[rows(r), cols(h)]
            ds = (dot(d, v[0:w, cols(h)], 1, 1) * table[h, rows(r), 0:w]).astype(BF16)
            dscores[h, rows(r), 0:w] = ds
            inter = grow[rows(r), h : h + 1] * dot(d, state(fore_state, h), 1, 1)
            dq[rows(r), cols(h)] = (dot(ds, k[0:w, cols(h)], 1, 0) + inter).astype(BF16)
        for c in range(CHUNKS):
            later = slice(c * CHUNK, BLOCK)
            dk_part[rows(c), cols(h)] = dot(dscores[h, later, rows(c)], q[later, cols(h)], 0, 0)
            dv_part[rows(c), cols(h)] = dot(probs[h, later, rows(c)], dattn[later, cols(h)], 0, 0)

    for h in range(heads // 2):
        backward(h)
    arrived(gain_pair, GAIN_PAIR)
    gain_in[chip] = gain_own[...] + gain_pair[...]

    scan(back_up_in, back_down, back_whole, reversed(range(chips)), BACKWARD)
    for p in peers:
        send(gain_in.at[chip], gain_in.at[chip], GAIN, on_chip(p))

    for h in range(heads // 2, heads):
        backward(h)

    arrived(gain_in.at[pl.ds(0, chips - 1)], GAIN)
    total = gain_in[0]
    for j in range(1, chips):
        total = total + gain_in[j]
    dgain[...] = total

    settle(back_whole, back_pair, BACKWARD)
    for h in range(heads):
        back_state[pieces(h)] = entering(back_whole, back_pair, back_leads, h)

    sent(decay_own, DECAY_PAIR)
    sent(decay_in.at[pl.ds(0, chips - 1)], DECAY)
    sent(arriving, GRAD)
    sent(norm_in.at[pl.ds(0, m - 1)], NORM)
    sent(gain_own, GAIN_PAIR)
    sent(gain_in.at[pl.ds(0, chips - 1)], GAIN)
    for first, up_out in ((FORWARD, fore_up_out), (BACKWARD, back_up_out)):
        one_less = up_out.at[pl.ds(0, chips - 1)]
        for which, some in ((URGENT, up_out), (REST, up_out), (UP, one_less), (DOWN, one_less), (WHOLE, up_out)):
            sent(some, first + which)


def finish(
    dq, dgate, dgain, k, v, shrink, back_state, dk_part, dv_part,
    dq_hbm, dgate_hbm, dgain_hbm, dk_hbm, dv_hbm,
    dk, dv, sem,
):
    heads = dgain.shape[0]
    per_head = back_state.shape[0] // heads
    copies = [
        pltpu.make_async_copy(src, dst, sem.at[i])
        for i, (src, dst) in enumerate(((dq, dq_hbm), (dgate, dgate_hbm), (dgain, dgain_hbm)))
    ]
    for copy in copies:
        copy.start()
    for h in range(heads):
        cols = slice(h * HEAD, (h + 1) * HEAD)
        back = back_state[h * per_head : (h + 1) * per_head].reshape(HEAD, HEAD)
        fade = shrink[:, h : h + 1]
        for i, (part, other, over, out, out_hbm) in enumerate(
            ((dk_part, v, 1, dk, dk_hbm), (dv_part, k, 0, dv, dv_hbm))
        ):
            out[:, cols] = (part[:, cols] + fade * dot(other[:, cols], back, 1, over)).astype(BF16)
            copies.append(pltpu.make_async_copy(out.at[:, cols], out_hbm.at[:, cols], sem.at[3 + 2 * h + i]))
            copies[-1].start()
    for copy in copies:
        copy.wait()


def local(n, m, queries, keys, values, log_decay, gate, gain, grad_out):
    heads = queries.shape[1] // HEAD
    width = heads * HEAD
    assert queries.shape[0] == BLOCK and n % heads == 0
    piece = (heads * HEAD // n, HEAD)
    square = (BLOCK, width)
    pairs = (heads, BLOCK, BLOCK)
    vmem = pltpu.VMEM
    sweep = [
        vmem((n, *piece), F32), *[vmem((n, *piece), BF16)] * 2,
        *[vmem((n // 2, *piece), BF16)] * 3, vmem((n, *piece), BF16),
    ]
    outs = pl.pallas_call(
        functools.partial(kernel, n, m, heads),
        out_shape=[
            jax.ShapeDtypeStruct(shape, kind)
            for shape, kind in (
                (square, BF16), (square, BF16), ((heads, HEAD), F32), (square, BF16), (square, BF16),
                ((BLOCK, 16), F32), ((n, *piece), BF16), (square, F32), (square, F32),
            )
        ],
        in_specs=[pl.BlockSpec(memory_space=pltpu.HBM)] * 7,
        out_specs=[pl.BlockSpec(memory_space=pltpu.VMEM)] * 9,
        scratch_shapes=[
            vmem((heads, BLOCK), F32), vmem((heads, HEAD), F32),
            *[vmem(square, BF16)] * 3,
            vmem((16, BLOCK), F32), vmem((BLOCK, BLOCK), BF16),
            vmem((BLOCK, 16), F32), vmem((16, BLOCK), F32), vmem((BLOCK, 16), F32),
            vmem(pairs, F32), vmem(pairs, BF16), vmem(pairs, BF16),
            *[vmem(square, F32)] * 3, vmem(square, BF16), *[vmem((width, BLOCK), BF16)] * 2,
            *[vmem((heads, 1, HEAD), F32)] * 3, vmem((n // 2, 1, HEAD), F32),
            vmem((2 * CHUNKS, CHUNK), F32), vmem((m, 2 * CHUNKS, CHUNK), F32),
            vmem((CHUNK, CHUNK), F32), vmem((CHUNK, CHUNK), F32),
            *[vmem((heads, HEAD), F32)] * 2, vmem((n // 2, heads, HEAD), F32),
            *sweep, vmem((n, *piece), BF16),
            *sweep,
            pltpu.SemaphoreType.DMA((7,)),
            pltpu.SemaphoreType.DMA((SEMAPHORES,)), pltpu.SemaphoreType.DMA((SEMAPHORES,)),
        ],
        compiler_params=pltpu.CompilerParams(
            collective_id=0, has_side_effects=True, vmem_limit_bytes=40 << 20
        ),
    )(*[pltpu.with_memory_space_constraint(x, pltpu.HBM) for x in (log_decay, gain.reshape(heads, HEAD), keys, values, queries, gate, grad_out)])
    dq, dgate, dgain, dk, dv = pl.pallas_call(
        finish,
        out_shape=[jax.ShapeDtypeStruct(x.shape, x.dtype) for x in (*outs[:3], *outs[:2])],
        in_specs=[pl.BlockSpec(memory_space=pltpu.VMEM)] * len(outs),
        out_specs=[pl.BlockSpec(memory_space=pltpu.HBM)] * 5,
        scratch_shapes=[*[vmem(square, BF16)] * 2, pltpu.SemaphoreType.DMA((3 + 2 * heads,))],
        compiler_params=pltpu.CompilerParams(vmem_limit_bytes=16 << 20),
    )(*[pltpu.with_memory_space_constraint(x, pltpu.VMEM) for x in outs])
    return dq, dk, dv, dgate, dgain.reshape(width)


def solution(mesh):
    return jax.shard_map(
        functools.partial(local, mesh.shape["ctx"], mesh.shape["tp"]),
        mesh=mesh,
        in_specs=(
            P("ctx", "tp"),
            P("ctx", "tp"),
            P("ctx", "tp"),
            P("tp", "ctx"),
            P("ctx", "tp"),
            P("tp"),
            P(("ctx", "tp"), None),
        ),
        out_specs=(P("ctx", "tp"), P("ctx", "tp"), P("ctx", "tp"), P("ctx", "tp"), P("tp")),
        check_vma=False,
    )
```

```python
import functools

import jax
import jax.numpy as jnp
from jax import lax
from jax.experimental import pallas as pl
from jax.experimental.pallas import tpu as pltpu
from jax.sharding import PartitionSpec as P

HEAD = 128
BLOCK = 512
CHUNK = 128
CHUNKS = BLOCK // CHUNK
EPSILON = 1e-06
MESH = pl.DeviceIdType.MESH
F32, BF16 = jnp.float32, jnp.bfloat16

DECAY_PAIR, DECAY, GRAD, NORM, GAIN_PAIR, GAIN, FORWARD, BACKWARD = 0, 1, 2, 3, 4, 5, 6, 10
URGENT, REST, UP, DOWN = range(4)
SEMAPHORES = 14


def dot(a, b, over_a, over_b):
    return lax.dot_general(
        a, b, (((over_a,), (over_b,)), ((), ())), preferred_element_type=F32
    )


def halves(x):
    high = x.astype(BF16)
    return high, (x - high.astype(F32)).astype(BF16)


def far_first(count):
    return sorted(range(count), key=lambda i: -min(i, count - i))


def kernel(
    n, m, heads,
    ld_hbm, gain_hbm, k_hbm, v_hbm, q_hbm, gate_hbm, grad_hbm,
    dq, dgate, dgain, k, v, shrink, back_state, dk_part, dv_part,
    ld, gain, q, gate, grad,
    ld_rows, tri, cum_col, cum_row, grow,
    table, probs, dscores, attention, dnorm, dscaled, closed, dattn, q_both,
    decay_own, decay_pair, decay_out, decay_in,
    norm_out, norm_in, coefs, columns, gain_own, gain_pair, gain_in,
    fore_own, fore_out, fore_pair, fore_up_out, fore_up_in, fore_down, fore_whole, fore_state,
    back_own, back_out, back_pair, back_up_out, back_up_in, back_down, back_whole,
    in_sem, send_sem, recv_sem,
):
    me, mt = lax.axis_index("ctx"), lax.axis_index("tp")
    core, chip = lax.rem(me, 2), me // 2
    chips, deep = n // 2, n // 4
    slices = chips // 2
    per_head = 2 * slices // heads
    channels = heads * HEAD * m
    width = heads * HEAD
    grad_rows = BLOCK // m
    half = pl.ds(core * slices, slices)
    other_half = pl.ds((1 - core) * slices, slices)

    loads = [
        pltpu.make_async_copy(src, dst, in_sem.at[i])
        for i, (src, dst) in enumerate(
            ((ld_hbm, ld), (k_hbm, k), (v_hbm, v), (q_hbm, q), (gate_hbm, gate), (gain_hbm, gain))
        )
    ]
    for load in loads:
        load.start()

    def chip_at(y, z):
        return lax.rem(chip // deep + y, 2) * deep + lax.rem(chip + z + deep, deep)

    peers = [chip_at(y, z) for z in far_first(deep) for y in (1, 0) if (y, z) != (0, 0)]
    near = sorted(range(1 - deep // 4, deep // 4 + 1), key=lambda z: -abs(z))
    served = [(y, z, c) for z in near for y in (1, 0) for c in (0, 1) if (y, z, c) != (0, 0, 0)]
    across = [(y, z) for z in range(-(deep // 4), deep // 4 + 1) for y in (1, 0) if (y, z) != (0, 0)]
    tp_peers = [
        lax.rem(mt // 2 + x, m // 2) * 2 + lax.rem(mt + y, 2)
        for y in (1, 0)
        for x in far_first(m // 2)
        if (y, x) != (0, 0)
    ]

    def on_chip(p):
        return {"ctx": 2 * p + core, "tp": mt}

    def on_tp(p):
        return {"ctx": me, "tp": p}

    sibling = {"ctx": 2 * chip + 1 - core, "tp": mt}

    barrier = pltpu.get_barrier_semaphore()
    greeted = [on_chip(p) for p in peers] + [on_tp(p) for p in tp_peers] + [sibling]
    greeted += [{"ctx": 2 * chip_at(y, z) + 1 - core, "tp": mt} for y, z in across]
    for device in greeted:
        pl.semaphore_signal(barrier, inc=1, device_id=device, device_id_type=MESH)

    def send(src, dst, which, device):
        pltpu.make_async_remote_copy(
            src_ref=src,
            dst_ref=dst,
            send_sem=send_sem.at[which],
            recv_sem=recv_sem.at[which],
            device_id=device,
            device_id_type=MESH,
        ).start()

    def arrived(some, which):
        pltpu.make_async_copy(some, some, recv_sem.at[which]).wait()

    def sent(some, which):
        pltpu.make_async_copy(some, some, send_sem.at[which]).wait()

    def cols(h):
        return slice(h * HEAD, (h + 1) * HEAD)

    def rows(r):
        return slice(r * CHUNK, (r + 1) * CHUNK)

    def pieces(h):
        return slice(h * per_head, (h + 1) * per_head)

    def state(ref, h):
        return ref[pieces(h)].reshape(HEAD, HEAD)

    def slice_of(p):
        return (p // deep) * (deep // 2) + lax.rem(p, deep // 2)

    mine = core * slices + slice_of(chip)

    t = lax.broadcasted_iota(jnp.int32, (BLOCK, BLOCK), 0)
    u = lax.broadcasted_iota(jnp.int32, (BLOCK, BLOCK), 1)
    tri[...] = jnp.where(t >= u, 1.0, 0.0).astype(BF16)
    ld_rows[...] = jnp.zeros_like(ld_rows)
    coefs[...] = jnp.zeros_like(coefs)
    loads[0].wait()
    ld_rows[0:heads, :] = ld[...]
    whole = ld_rows[...]
    part0 = whole.astype(BF16)
    rest = whole - part0.astype(F32)
    part1 = rest.astype(BF16)
    part2 = (rest - part1.astype(F32)).astype(BF16)
    col = dot(tri[...], part0, 1, 1) + dot(tri[...], part1, 1, 1) + dot(tri[...], part2, 1, 1)
    cum_col[...] = col
    last = col[BLOCK - 1 : BLOCK, :]
    grow[...] = jnp.exp(col)
    shrink[...] = jnp.exp(last - col)
    for h in range(heads):
        decay_own[h] = jnp.broadcast_to(jnp.exp(last[:, h : h + 1]), (1, HEAD))

    def share(h, addend, own, out):
        addend = addend.reshape(per_head, HEAD // per_head, HEAD)
        own[pieces(h)] = addend
        out[pieces(h)] = addend.astype(BF16)

    def swap(out, pair, first):
        send(out.at[other_half], pair.at[other_half], first + URGENT, sibling)
        send(out.at[half], pair.at[half], first + REST, sibling)

    def join(own, pair, up_out, up_in, leads, first):
        arrived(pair.at[half], first + URGENT)
        for g in range(heads // 2):
            h = core * (heads // 2) + g
            here = pl.ds(core * slices + g * per_head, per_head)
            by_own = leads * decay_pair[h] + (1.0 - leads)
            by_pair = leads + (1.0 - leads) * decay_own[h]
            up_out[pieces(g)] = (own[here] * by_own + pair[here].astype(F32) * by_pair).astype(BF16)
        for p in peers:
            send(up_out.at[slice_of(p)], up_in.at[chip], first + UP, on_chip(p))
        up_in[chip] = up_out[slice_of(chip)]

    def scan(up_in, down, whole, order, first):
        arrived(up_in.at[pl.ds(0, chips - 1)], first + UP)
        carried = jnp.zeros(up_in.shape[1:], F32)
        for j in order:
            down[j] = carried.astype(BF16)
            carried = carried * decay_in[j] + up_in[j].astype(F32)
        for y, z, c in served:
            p = chip_at(y, z * (1 - 2 * core))
            send(down.at[p], whole.at[mine], first + DOWN, {"ctx": 2 * p + lax.rem(core + c, 2), "tp": mt})
        whole[mine] = down[chip]

    def settle(whole, pair, first):
        arrived(pair.at[other_half], first + REST)
        arrived(whole.at[pl.ds(0, len(served))], first + DOWN)

    def entering(whole, pair, leads, h):
        by_chip = leads + (1.0 - leads) * decay_pair[h]
        held = whole[pieces(h)].astype(F32) * by_chip + pair[pieces(h)].astype(F32) * (1.0 - leads)
        return held.astype(BF16)

    fore_leads = (1 - core).astype(F32)
    back_leads = core.astype(F32)

    loads[1].wait()
    loads[2].wait()
    for h in range(heads):
        high, low = halves(k[:, cols(h)].astype(F32) * shrink[:, h : h + 1])
        share(h, dot(high, v[:, cols(h)], 0, 0) + dot(low, v[:, cols(h)], 0, 0), fore_own, fore_out)
    pl.semaphore_wait(barrier, len(greeted))
    send(decay_own, decay_pair, DECAY_PAIR, sibling)
    swap(fore_out, fore_pair, FORWARD)

    def grad_part(p):
        return grad_hbm.at[:, pl.ds(pl.multiple_of(p * width, width), width)]

    grad_place = grad.at[pl.ds(pl.multiple_of(mt * grad_rows, grad_rows), grad_rows), :]
    own_grad = pltpu.make_async_copy(grad_part(mt), grad_place, in_sem.at[6])
    own_grad.start()
    for p in tp_peers:
        send(grad_part(p), grad_place, GRAD, on_tp(p))

    arrived(decay_pair, DECAY_PAIR)
    decay_out[...] = decay_own[...] * decay_pair[...]
    for p in peers:
        send(decay_out.at[(core * slices + slice_of(p)) // per_head], decay_in.at[chip], DECAY, on_chip(p))
    decay_in[chip] = decay_out[mine // per_head]
    join(fore_own, fore_pair, fore_up_out, fore_up_in, fore_leads, FORWARD)

    cum_row[...] = dot(part0, tri[...], 1, 1) + dot(part1, tri[...], 1, 1) + dot(part2, tri[...], 1, 1)
    loads[3].wait()

    def inside(h):
        for r in range(CHUNKS):
            w = (r + 1) * CHUNK
            scores = dot(q[rows(r), cols(h)], k[0:w, cols(h)], 1, 1)
            spread = cum_col[rows(r), h : h + 1] - cum_row[h : h + 1, 0:w]
            at = lax.broadcasted_iota(jnp.int32, (CHUNK, w), 0) + r * CHUNK
            weight = jnp.where(
                at >= lax.broadcasted_iota(jnp.int32, (CHUNK, w), 1),
                jnp.exp(jnp.minimum(spread, 0.0)),
                0.0,
            )
            table[h, rows(r), 0:w] = weight
            p = (scores * weight).astype(BF16)
            probs[h, rows(r), 0:w] = p
            attention[rows(r), cols(h)] = dot(p, v[0:w, cols(h)], 1, 0)
        high, low = halves(q[:, cols(h)].astype(F32) * grow[:, h : h + 1])
        q_both[h, 0:HEAD, :] = jnp.transpose(high)
        q_both[h, HEAD : 2 * HEAD, :] = jnp.transpose(low)

    for h in range(heads // 2):
        inside(h)

    arrived(decay_in.at[pl.ds(0, chips - 1)], DECAY)
    scan(fore_up_in, fore_down, fore_whole, range(chips), FORWARD)

    for h in range(heads // 2, heads):
        inside(h)
    loads[4].wait()
    loads[5].wait()
    own_grad.wait()
    arriving = grad.at[pl.ds(0, (m - 1) * grad_rows), :]
    arrived(arriving, GRAD)
    for r in range(CHUNKS):
        for h in range(heads):
            opened = jax.nn.sigmoid(gate[rows(r), cols(h)].astype(F32))
            d = grad[rows(r), cols(h)].astype(F32) * opened
            dnorm[rows(r), cols(h)] = d
            dscaled[rows(r), cols(h)] = d * gain[h : h + 1, :]
            closed[rows(r), cols(h)] = 1.0 - opened

    settle(fore_whole, fore_pair, FORWARD)
    for h in range(heads):
        fore_state[pieces(h)] = entering(fore_whole, fore_pair, fore_leads, h)
    ones = jnp.ones((16, HEAD), BF16)
    for b in range(CHUNKS // 2):
        two = slice(2 * b * CHUNK, 2 * (b + 1) * CHUNK)
        squares = jnp.zeros((2 * CHUNK, HEAD), F32)
        inner = jnp.zeros((2 * CHUNK, HEAD), F32)
        for h in range(heads):
            a = attention[two, cols(h)] + grow[two, h : h + 1] * dot(
                q[two, cols(h)], state(fore_state, h), 1, 0
            )
            attention[two, cols(h)] = a
            squares = squares + a * a
            inner = inner + a * dscaled[two, cols(h)]
        for place, total in ((2 * b, squares), (CHUNKS + 2 * b, inner)):
            high, low = halves(total)
            line = dot(ones, high, 1, 1) + dot(ones, low, 1, 1)
            norm_out[place : place + 1, :] = line[0:1, 0:CHUNK]
            norm_out[place + 1 : place + 2, :] = line[0:1, CHUNK : 2 * CHUNK]
    for p in tp_peers:
        send(norm_out, norm_in.at[mt], NORM, on_tp(p))
    norm_in[mt] = norm_out[...]
    arrived(norm_in.at[pl.ds(0, m - 1)], NORM)
    total = norm_in[0]
    for j in range(1, m):
        total = total + norm_in[j]
    rscale = lax.rsqrt(total[0:CHUNKS] / channels + EPSILON)
    coefs[0:CHUNKS, :] = rscale
    coefs[CHUNKS : 2 * CHUNKS, :] = total[CHUNKS : 2 * CHUNKS] * (rscale * rscale * rscale) / channels
    columns[...] = jnp.transpose(coefs[...])

    for r in range(CHUNKS):
        scale, pull = columns[:, r : r + 1], columns[:, CHUNKS + r : CHUNKS + r + 1]
        for h in range(heads):
            d = dscaled[rows(r), cols(h)] * scale - attention[rows(r), cols(h)] * pull
            dattn[rows(r), cols(h)] = d.astype(BF16)
    for h in range(heads):
        both = dot(q_both[h], dattn[:, cols(h)], 1, 0)
        share(h, both[0:HEAD] + both[HEAD : 2 * HEAD], back_own, back_out)
    swap(back_out, back_pair, BACKWARD)

    for h in range(heads):
        part = jnp.zeros((1, HEAD), F32)
        for r in range(CHUNKS):
            x = dnorm[rows(r), cols(h)] * attention[rows(r), cols(h)] * columns[:, r : r + 1]
            dgate[rows(r), cols(h)] = (x * gain[h : h + 1, :] * closed[rows(r), cols(h)]).astype(BF16)
            part = part + jnp.sum(x, axis=0, keepdims=True)
        gain_own[h : h + 1, :] = part
    send(gain_own, gain_pair, GAIN_PAIR, sibling)
    join(back_own, back_pair, back_up_out, back_up_in, back_leads, BACKWARD)

    def backward(h):
        for r in range(CHUNKS):
            w = (r + 1) * CHUNK
            d = dattn[rows(r), cols(h)]
            ds = (dot(d, v[0:w, cols(h)], 1, 1) * table[h, rows(r), 0:w]).astype(BF16)
            dscores[h, rows(r), 0:w] = ds
            inter = grow[rows(r), h : h + 1] * dot(d, state(fore_state, h), 1, 1)
            dq[rows(r), cols(h)] = (dot(ds, k[0:w, cols(h)], 1, 0) + inter).astype(BF16)
        for c in range(CHUNKS):
            later = slice(c * CHUNK, BLOCK)
            dk_part[rows(c), cols(h)] = dot(dscores[h, later, rows(c)], q[later, cols(h)], 0, 0)
            dv_part[rows(c), cols(h)] = dot(probs[h, later, rows(c)], dattn[later, cols(h)], 0, 0)

    for h in range(heads // 2):
        backward(h)
    arrived(gain_pair, GAIN_PAIR)
    gain_in[chip] = gain_own[...] + gain_pair[...]

    scan(back_up_in, back_down, back_whole, reversed(range(chips)), BACKWARD)
    for p in peers:
        send(gain_in.at[chip], gain_in.at[chip], GAIN, on_chip(p))

    for h in range(heads // 2, heads):
        backward(h)

    arrived(gain_in.at[pl.ds(0, chips - 1)], GAIN)
    total = gain_in[0]
    for j in range(1, chips):
        total = total + gain_in[j]
    dgain[...] = total

    settle(back_whole, back_pair, BACKWARD)
    for h in range(heads):
        back_state[pieces(h)] = entering(back_whole, back_pair, back_leads, h)

    sent(decay_own, DECAY_PAIR)
    sent(decay_in.at[pl.ds(0, chips - 1)], DECAY)
    sent(arriving, GRAD)
    sent(norm_in.at[pl.ds(0, m - 1)], NORM)
    sent(gain_own, GAIN_PAIR)
    sent(gain_in.at[pl.ds(0, chips - 1)], GAIN)
    for first, up_out, up_in, whole in (
        (FORWARD, fore_up_out, fore_up_in, fore_whole),
        (BACKWARD, back_up_out, back_up_in, back_whole),
    ):
        sent(up_out, first + URGENT)
        sent(up_out, first + REST)
        sent(up_in.at[pl.ds(0, chips - 1)], first + UP)
        sent(whole.at[pl.ds(0, len(served))], first + DOWN)


def finish(
    dq, dgate, dgain, k, v, shrink, back_state, dk_part, dv_part,
    dq_hbm, dgate_hbm, dgain_hbm, dk_hbm, dv_hbm,
    dk, dv, sem,
):
    heads = dgain.shape[0]
    per_head = back_state.shape[0] // heads
    copies = [
        pltpu.make_async_copy(src, dst, sem.at[i])
        for i, (src, dst) in enumerate(((dq, dq_hbm), (dgate, dgate_hbm), (dgain, dgain_hbm)))
    ]
    for copy in copies:
        copy.start()
    for h in range(heads):
        cols = slice(h * HEAD, (h + 1) * HEAD)
        back = back_state[h * per_head : (h + 1) * per_head].reshape(HEAD, HEAD)
        fade = shrink[:, h : h + 1]
        for i, (part, other, over, out, out_hbm) in enumerate(
            ((dk_part, v, 1, dk, dk_hbm), (dv_part, k, 0, dv, dv_hbm))
        ):
            out[:, cols] = (part[:, cols] + fade * dot(other[:, cols], back, 1, over)).astype(BF16)
            copies.append(pltpu.make_async_copy(out.at[:, cols], out_hbm.at[:, cols], sem.at[3 + 2 * h + i]))
            copies[-1].start()
    for copy in copies:
        copy.wait()


def local(n, m, queries, keys, values, log_decay, gate, gain, grad_out):
    heads = queries.shape[1] // HEAD
    width = heads * HEAD
    assert queries.shape[0] == BLOCK and n % (2 * heads) == 0
    count = n // 2
    piece = (width // count, HEAD)
    square = (BLOCK, width)
    pairs = (heads, BLOCK, BLOCK)
    vmem = pltpu.VMEM
    sweep = [
        vmem((count, *piece), F32), *[vmem((count, *piece), BF16)] * 2,
        vmem((count // 2, *piece), BF16), *[vmem((n // 2, *piece), BF16)] * 2, vmem((count, *piece), BF16),
    ]
    outs = pl.pallas_call(
        functools.partial(kernel, n, m, heads),
        out_shape=[
            jax.ShapeDtypeStruct(shape, kind)
            for shape, kind in (
                (square, BF16), (square, BF16), ((heads, HEAD), F32), (square, BF16), (square, BF16),
                ((BLOCK, 16), F32), ((count, *piece), BF16), (square, F32), (square, F32),
            )
        ],
        in_specs=[pl.BlockSpec(memory_space=pltpu.HBM)] * 7,
        out_specs=[pl.BlockSpec(memory_space=pltpu.VMEM)] * 9,
        scratch_shapes=[
            vmem((heads, BLOCK), F32), vmem((heads, HEAD), F32),
            *[vmem(square, BF16)] * 3,
            vmem((16, BLOCK), F32), vmem((BLOCK, BLOCK), BF16),
            vmem((BLOCK, 16), F32), vmem((16, BLOCK), F32), vmem((BLOCK, 16), F32),
            vmem(pairs, F32), vmem(pairs, BF16), vmem(pairs, BF16),
            *[vmem(square, F32)] * 4, vmem(square, BF16), vmem((heads, 2 * HEAD, BLOCK), BF16),
            *[vmem((heads, 1, HEAD), F32)] * 3, vmem((n // 2, 1, HEAD), F32),
            vmem((2 * CHUNKS, CHUNK), F32), vmem((m, 2 * CHUNKS, CHUNK), F32),
            vmem((CHUNK, CHUNK), F32), vmem((CHUNK, CHUNK), F32),
            *[vmem((heads, HEAD), F32)] * 2, vmem((n // 2, heads, HEAD), F32),
            *sweep, vmem((count, *piece), BF16),
            *sweep,
            pltpu.SemaphoreType.DMA((7,)),
            pltpu.SemaphoreType.DMA((SEMAPHORES,)), pltpu.SemaphoreType.DMA((SEMAPHORES,)),
        ],
        compiler_params=pltpu.CompilerParams(
            collective_id=0, has_side_effects=True, vmem_limit_bytes=40 << 20
        ),
    )(*[pltpu.with_memory_space_constraint(x, pltpu.HBM) for x in (log_decay, gain.reshape(heads, HEAD), keys, values, queries, gate, grad_out)])
    dq, dgate, dgain, dk, dv = pl.pallas_call(
        finish,
        out_shape=[jax.ShapeDtypeStruct(x.shape, x.dtype) for x in (*outs[:3], *outs[:2])],
        in_specs=[pl.BlockSpec(memory_space=pltpu.VMEM)] * len(outs),
        out_specs=[pl.BlockSpec(memory_space=pltpu.HBM)] * 5,
        scratch_shapes=[*[vmem(square, BF16)] * 2, pltpu.SemaphoreType.DMA((3 + 2 * heads,))],
        compiler_params=pltpu.CompilerParams(vmem_limit_bytes=16 << 20),
    )(*[pltpu.with_memory_space_constraint(x, pltpu.VMEM) for x in outs])
    return dq, dk, dv, dgate, dgain.reshape(width)


def solution(mesh):
    return jax.shard_map(
        functools.partial(local, mesh.shape["ctx"], mesh.shape["tp"]),
        mesh=mesh,
        in_specs=(
            P("ctx", "tp"),
            P("ctx", "tp"),
            P("ctx", "tp"),
            P("tp", "ctx"),
            P("ctx", "tp"),
            P("tp"),
            P(("ctx", "tp"), None),
        ),
        out_specs=(P("ctx", "tp"), P("ctx", "tp"), P("ctx", "tp"), P("ctx", "tp"), P("tp")),
        check_vma=False,
    )
```

```python
import functools

import jax
import jax.numpy as jnp
from jax import lax
from jax.experimental import pallas as pl
from jax.experimental.pallas import tpu as pltpu
from jax.sharding import PartitionSpec as P

HEAD = 128
BLOCK = 512
CHUNK = 128
CHUNKS = BLOCK // CHUNK
EPSILON = 1e-06
MESH = pl.DeviceIdType.MESH
F32, BF16 = jnp.float32, jnp.bfloat16

DECAY_PAIR, DECAY, GRAD, NORM, GAIN_PAIR, GAIN, FORWARD, BACKWARD = 0, 1, 2, 3, 4, 5, 6, 10
URGENT, REST, UP, DOWN = range(4)
SEMAPHORES = 14


def dot(a, b, over_a, over_b):
    return lax.dot_general(
        a, b, (((over_a,), (over_b,)), ((), ())), preferred_element_type=F32
    )


def halves(x):
    high = x.astype(BF16)
    return high, (x - high.astype(F32)).astype(BF16)


def far_first(count):
    return sorted(range(count), key=lambda i: -min(i, count - i))


def kernel(
    n, m, heads,
    ld_hbm, gain_hbm, k_hbm, v_hbm, q_hbm, gate_hbm, grad_hbm,
    dq, dgate, dgain, k, v, shrink, back_state, dk_part, dv_part,
    ld, gain, q, gate, grad,
    ld_rows, tri, cum_col, cum_row, grow,
    table, probs, dscores, attention, dnorm, dscaled, closed, dattn, q_both,
    decay_own, decay_pair, decay_out, decay_in,
    norm_out, norm_in, coefs, columns, gain_own, gain_pair, gain_in,
    fore_own, fore_out, fore_pair, fore_up_out, fore_up_in, fore_down, fore_whole, fore_state,
    back_own, back_out, back_pair, back_up_out, back_up_in, back_down, back_whole,
    in_sem, send_sem, recv_sem,
):
    me, mt = lax.axis_index("ctx"), lax.axis_index("tp")
    core, chip = lax.rem(me, 2), me // 2
    chips, deep = n // 2, n // 4
    slices = chips // 2
    per_head = 2 * slices // heads
    channels = heads * HEAD * m
    width = heads * HEAD
    grad_rows = BLOCK // m
    half = pl.ds(core * slices, slices)
    other_half = pl.ds((1 - core) * slices, slices)

    loads = [
        pltpu.make_async_copy(src, dst, in_sem.at[i])
        for i, (src, dst) in enumerate(
            ((ld_hbm, ld), (k_hbm, k), (v_hbm, v), (q_hbm, q), (gate_hbm, gate), (gain_hbm, gain))
        )
    ]
    for load in loads:
        load.start()

    def chip_at(y, z):
        return lax.rem(chip // deep + y, 2) * deep + lax.rem(chip + z + deep, deep)

    peers = [chip_at(y, z) for z in far_first(deep) for y in (1, 0) if (y, z) != (0, 0)]
    near = sorted(range(1 - deep // 4, deep // 4 + 1), key=lambda z: -abs(z))
    served = [(y, z, c) for z in near for y in (1, 0) for c in (0, 1) if (y, z, c) != (0, 0, 0)]
    across = [(y, z) for z in range(-(deep // 4), deep // 4 + 1) for y in (1, 0) if (y, z) != (0, 0)]
    tp_peers = [
        lax.rem(mt // 2 + x, m // 2) * 2 + lax.rem(mt + y, 2)
        for y in (1, 0)
        for x in far_first(m // 2)
        if (y, x) != (0, 0)
    ]

    def on_chip(p):
        return {"ctx": 2 * p + core, "tp": mt}

    def on_tp(p):
        return {"ctx": me, "tp": p}

    sibling = {"ctx": 2 * chip + 1 - core, "tp": mt}

    barrier = pltpu.get_barrier_semaphore()
    greeted = [on_chip(p) for p in peers] + [on_tp(p) for p in tp_peers] + [sibling]
    greeted += [{"ctx": 2 * chip_at(y, z) + 1 - core, "tp": mt} for y, z in across]
    for device in greeted:
        pl.semaphore_signal(barrier, inc=1, device_id=device, device_id_type=MESH)

    def send(src, dst, which, device):
        pltpu.make_async_remote_copy(
            src_ref=src,
            dst_ref=dst,
            send_sem=send_sem.at[which],
            recv_sem=recv_sem.at[which],
            device_id=device,
            device_id_type=MESH,
        ).start()

    def arrived(some, which):
        pltpu.make_async_copy(some, some, recv_sem.at[which]).wait()

    def sent(some, which):
        pltpu.make_async_copy(some, some, send_sem.at[which]).wait()

    def cols(h):
        return slice(h * HEAD, (h + 1) * HEAD)

    def rows(r):
        return slice(r * CHUNK, (r + 1) * CHUNK)

    def pieces(h):
        return slice(h * per_head, (h + 1) * per_head)

    def state(ref, h):
        return ref[pieces(h)].reshape(HEAD, HEAD)

    def slice_of(p):
        return (p // deep) * (deep // 2) + lax.rem(p, deep // 2)

    mine = core * slices + slice_of(chip)

    t = lax.broadcasted_iota(jnp.int32, (BLOCK, BLOCK), 0)
    u = lax.broadcasted_iota(jnp.int32, (BLOCK, BLOCK), 1)
    tri[...] = jnp.where(t >= u, 1.0, 0.0).astype(BF16)
    ld_rows[...] = jnp.zeros_like(ld_rows)
    coefs[...] = jnp.zeros_like(coefs)
    loads[0].wait()
    ld_rows[0:heads, :] = ld[...]
    whole = ld_rows[...]
    part0 = whole.astype(BF16)
    rest = whole - part0.astype(F32)
    part1 = rest.astype(BF16)
    part2 = (rest - part1.astype(F32)).astype(BF16)
    col = dot(tri[...], part0, 1, 1) + dot(tri[...], part1, 1, 1) + dot(tri[...], part2, 1, 1)
    cum_col[...] = col
    last = col[BLOCK - 1 : BLOCK, :]
    grow[...] = jnp.exp(col)
    shrink[...] = jnp.exp(last - col)
    for h in range(heads):
        decay_own[h] = jnp.broadcast_to(jnp.exp(last[:, h : h + 1]), (1, HEAD))

    def share(h, addend, own, out):
        addend = addend.reshape(per_head, HEAD // per_head, HEAD)
        own[pieces(h)] = addend
        out[pieces(h)] = addend.astype(BF16)

    def swap(out, pair, first):
        send(out.at[other_half], pair.at[other_half], first + URGENT, sibling)
        send(out.at[half], pair.at[half], first + REST, sibling)

    def join(own, pair, up_out, up_in, leads, first):
        arrived(pair.at[half], first + URGENT)
        for g in range(heads // 2):
            h = core * (heads // 2) + g
            here = pl.ds(core * slices + g * per_head, per_head)
            by_own = leads * decay_pair[h] + (1.0 - leads)
            by_pair = leads + (1.0 - leads) * decay_own[h]
            up_out[pieces(g)] = (own[here] * by_own + pair[here].astype(F32) * by_pair).astype(BF16)
        for p in peers:
            send(up_out.at[slice_of(p)], up_in.at[chip], first + UP, on_chip(p))
        up_in[chip] = up_out[slice_of(chip)]

    def scan(up_in, down, whole, order, first):
        arrived(up_in.at[pl.ds(0, chips - 1)], first + UP)
        carried = jnp.zeros(up_in.shape[1:], F32)
        for j in order:
            down[j] = carried.astype(BF16)
            carried = carried * decay_in[j] + up_in[j].astype(F32)
        for y, z, c in served:
            p = chip_at(y, z * (1 - 2 * core))
            send(down.at[p], whole.at[mine], first + DOWN, {"ctx": 2 * p + lax.rem(core + c, 2), "tp": mt})
        whole[mine] = down[chip]

    def settle(whole, pair, first):
        arrived(pair.at[other_half], first + REST)
        arrived(whole.at[pl.ds(0, len(served))], first + DOWN)

    def entering(whole, pair, leads, h):
        by_chip = leads + (1.0 - leads) * decay_pair[h]
        held = whole[pieces(h)].astype(F32) * by_chip + pair[pieces(h)].astype(F32) * (1.0 - leads)
        return held.astype(BF16)

    fore_leads = (1 - core).astype(F32)
    back_leads = core.astype(F32)

    loads[1].wait()
    loads[2].wait()
    for h in range(heads):
        high, low = halves(k[:, cols(h)].astype(F32) * shrink[:, h : h + 1])
        share(h, dot(high, v[:, cols(h)], 0, 0) + dot(low, v[:, cols(h)], 0, 0), fore_own, fore_out)
    pl.semaphore_wait(barrier, len(greeted))
    send(decay_own, decay_pair, DECAY_PAIR, sibling)
    swap(fore_out, fore_pair, FORWARD)

    arrived(decay_pair, DECAY_PAIR)
    decay_out[...] = decay_own[...] * decay_pair[...]
    for p in peers:
        send(decay_out.at[(core * slices + slice_of(p)) // per_head], decay_in.at[chip], DECAY, on_chip(p))
    decay_in[chip] = decay_out[mine // per_head]
    join(fore_own, fore_pair, fore_up_out, fore_up_in, fore_leads, FORWARD)

    def grad_part(p):
        return grad_hbm.at[:, pl.ds(pl.multiple_of(p * width, width), width)]

    grad_place = grad.at[pl.ds(pl.multiple_of(mt * grad_rows, grad_rows), grad_rows), :]
    own_grad = pltpu.make_async_copy(grad_part(mt), grad_place, in_sem.at[6])
    own_grad.start()
    for p in tp_peers:
        send(grad_part(p), grad_place, GRAD, on_tp(p))


    cum_row[...] = dot(part0, tri[...], 1, 1) + dot(part1, tri[...], 1, 1) + dot(part2, tri[...], 1, 1)
    loads[3].wait()

    def inside(h):
        for r in range(CHUNKS):
            w = (r + 1) * CHUNK
            scores = dot(q[rows(r), cols(h)], k[0:w, cols(h)], 1, 1)
            spread = cum_col[rows(r), h : h + 1] - cum_row[h : h + 1, 0:w]
            at = lax.broadcasted_iota(jnp.int32, (CHUNK, w), 0) + r * CHUNK
            weight = jnp.where(
                at >= lax.broadcasted_iota(jnp.int32, (CHUNK, w), 1),
                jnp.exp(jnp.minimum(spread, 0.0)),
                0.0,
            )
            table[h, rows(r), 0:w] = weight
            p = (scores * weight).astype(BF16)
            probs[h, rows(r), 0:w] = p
            attention[rows(r), cols(h)] = dot(p, v[0:w, cols(h)], 1, 0)
        high, low = halves(q[:, cols(h)].astype(F32) * grow[:, h : h + 1])
        q_both[h, 0:HEAD, :] = jnp.transpose(high)
        q_both[h, HEAD : 2 * HEAD, :] = jnp.transpose(low)

    for h in range(heads // 2):
        inside(h)

    arrived(decay_in.at[pl.ds(0, chips - 1)], DECAY)
    scan(fore_up_in, fore_down, fore_whole, range(chips), FORWARD)

    for h in range(heads // 2, heads):
        inside(h)
    loads[4].wait()
    loads[5].wait()
    own_grad.wait()
    arriving = grad.at[pl.ds(0, (m - 1) * grad_rows), :]
    arrived(arriving, GRAD)
    for r in range(CHUNKS):
        for h in range(heads):
            opened = jax.nn.sigmoid(gate[rows(r), cols(h)].astype(F32))
            d = grad[rows(r), cols(h)].astype(F32) * opened
            dnorm[rows(r), cols(h)] = d
            dscaled[rows(r), cols(h)] = d * gain[h : h + 1, :]
            closed[rows(r), cols(h)] = 1.0 - opened

    settle(fore_whole, fore_pair, FORWARD)
    for h in range(heads):
        fore_state[pieces(h)] = entering(fore_whole, fore_pair, fore_leads, h)
    ones = jnp.ones((16, HEAD), BF16)
    for b in range(CHUNKS // 2):
        two = slice(2 * b * CHUNK, 2 * (b + 1) * CHUNK)
        squares = jnp.zeros((2 * CHUNK, HEAD), F32)
        inner = jnp.zeros((2 * CHUNK, HEAD), F32)
        for h in range(heads):
            a = attention[two, cols(h)] + grow[two, h : h + 1] * dot(
                q[two, cols(h)], state(fore_state, h), 1, 0
            )
            attention[two, cols(h)] = a
            squares = squares + a * a
            inner = inner + a * dscaled[two, cols(h)]
        for place, total in ((2 * b, squares), (CHUNKS + 2 * b, inner)):
            high, low = halves(total)
            line = dot(ones, high, 1, 1) + dot(ones, low, 1, 1)
            norm_out[place : place + 1, :] = line[0:1, 0:CHUNK]
            norm_out[place + 1 : place + 2, :] = line[0:1, CHUNK : 2 * CHUNK]
    for p in tp_peers:
        send(norm_out, norm_in.at[mt], NORM, on_tp(p))
    norm_in[mt] = norm_out[...]
    arrived(norm_in.at[pl.ds(0, m - 1)], NORM)
    total = norm_in[0]
    for j in range(1, m):
        total = total + norm_in[j]
    rscale = lax.rsqrt(total[0:CHUNKS] / channels + EPSILON)
    coefs[0:CHUNKS, :] = rscale
    coefs[CHUNKS : 2 * CHUNKS, :] = total[CHUNKS : 2 * CHUNKS] * (rscale * rscale * rscale) / channels
    columns[...] = jnp.transpose(coefs[...])

    for r in range(CHUNKS):
        scale, pull = columns[:, r : r + 1], columns[:, CHUNKS + r : CHUNKS + r + 1]
        for h in range(heads):
            d = dscaled[rows(r), cols(h)] * scale - attention[rows(r), cols(h)] * pull
            dattn[rows(r), cols(h)] = d.astype(BF16)
    for h in range(heads):
        both = dot(q_both[h], dattn[:, cols(h)], 1, 0)
        share(h, both[0:HEAD] + both[HEAD : 2 * HEAD], back_own, back_out)
    swap(back_out, back_pair, BACKWARD)

    for h in range(heads):
        part = jnp.zeros((1, HEAD), F32)
        for r in range(CHUNKS):
            x = dnorm[rows(r), cols(h)] * attention[rows(r), cols(h)] * columns[:, r : r + 1]
            dgate[rows(r), cols(h)] = (x * gain[h : h + 1, :] * closed[rows(r), cols(h)]).astype(BF16)
            part = part + jnp.sum(x, axis=0, keepdims=True)
        gain_own[h : h + 1, :] = part
    send(gain_own, gain_pair, GAIN_PAIR, sibling)
    join(back_own, back_pair, back_up_out, back_up_in, back_leads, BACKWARD)

    def backward(h):
        for r in range(CHUNKS):
            w = (r + 1) * CHUNK
            d = dattn[rows(r), cols(h)]
            ds = (dot(d, v[0:w, cols(h)], 1, 1) * table[h, rows(r), 0:w]).astype(BF16)
            dscores[h, rows(r), 0:w] = ds
            inter = grow[rows(r), h : h + 1] * dot(d, state(fore_state, h), 1, 1)
            dq[rows(r), cols(h)] = (dot(ds, k[0:w, cols(h)], 1, 0) + inter).astype(BF16)
        for c in range(CHUNKS):
            later = slice(c * CHUNK, BLOCK)
            dk_part[rows(c), cols(h)] = dot(dscores[h, later, rows(c)], q[later, cols(h)], 0, 0)
            dv_part[rows(c), cols(h)] = dot(probs[h, later, rows(c)], dattn[later, cols(h)], 0, 0)

    for h in range(heads // 2):
        backward(h)
    arrived(gain_pair, GAIN_PAIR)
    gain_in[chip] = gain_own[...] + gain_pair[...]

    scan(back_up_in, back_down, back_whole, reversed(range(chips)), BACKWARD)
    for p in peers:
        send(gain_in.at[chip], gain_in.at[chip], GAIN, on_chip(p))

    for h in range(heads // 2, heads):
        backward(h)

    arrived(gain_in.at[pl.ds(0, chips - 1)], GAIN)
    total = gain_in[0]
    for j in range(1, chips):
        total = total + gain_in[j]
    dgain[...] = total

    settle(back_whole, back_pair, BACKWARD)
    for h in range(heads):
        back_state[pieces(h)] = entering(back_whole, back_pair, back_leads, h)

    sent(decay_own, DECAY_PAIR)
    sent(decay_in.at[pl.ds(0, chips - 1)], DECAY)
    sent(arriving, GRAD)
    sent(norm_in.at[pl.ds(0, m - 1)], NORM)
    sent(gain_own, GAIN_PAIR)
    sent(gain_in.at[pl.ds(0, chips - 1)], GAIN)
    for first, up_out, up_in, whole in (
        (FORWARD, fore_up_out, fore_up_in, fore_whole),
        (BACKWARD, back_up_out, back_up_in, back_whole),
    ):
        sent(up_out, first + URGENT)
        sent(up_out, first + REST)
        sent(up_in.at[pl.ds(0, chips - 1)], first + UP)
        sent(whole.at[pl.ds(0, len(served))], first + DOWN)


def finish(
    dq, dgate, dgain, k, v, shrink, back_state, dk_part, dv_part,
    dq_hbm, dgate_hbm, dgain_hbm, dk_hbm, dv_hbm,
    dk, dv, sem,
):
    heads = dgain.shape[0]
    per_head = back_state.shape[0] // heads
    copies = [
        pltpu.make_async_copy(src, dst, sem.at[i])
        for i, (src, dst) in enumerate(((dq, dq_hbm), (dgate, dgate_hbm), (dgain, dgain_hbm)))
    ]
    for copy in copies:
        copy.start()
    for h in range(heads):
        cols = slice(h * HEAD, (h + 1) * HEAD)
        back = back_state[h * per_head : (h + 1) * per_head].reshape(HEAD, HEAD)
        fade = shrink[:, h : h + 1]
        for i, (part, other, over, out, out_hbm) in enumerate(
            ((dk_part, v, 1, dk, dk_hbm), (dv_part, k, 0, dv, dv_hbm))
        ):
            out[:, cols] = (part[:, cols] + fade * dot(other[:, cols], back, 1, over)).astype(BF16)
            copies.append(pltpu.make_async_copy(out.at[:, cols], out_hbm.at[:, cols], sem.at[3 + 2 * h + i]))
            copies[-1].start()
    for copy in copies:
        copy.wait()


def local(n, m, queries, keys, values, log_decay, gate, gain, grad_out):
    heads = queries.shape[1] // HEAD
    width = heads * HEAD
    assert queries.shape[0] == BLOCK and n % (2 * heads) == 0
    count = n // 2
    piece = (width // count, HEAD)
    square = (BLOCK, width)
    pairs = (heads, BLOCK, BLOCK)
    vmem = pltpu.VMEM
    sweep = [
        vmem((count, *piece), F32), *[vmem((count, *piece), BF16)] * 2,
        vmem((count // 2, *piece), BF16), *[vmem((n // 2, *piece), BF16)] * 2, vmem((count, *piece), BF16),
    ]
    outs = pl.pallas_call(
        functools.partial(kernel, n, m, heads),
        out_shape=[
            jax.ShapeDtypeStruct(shape, kind)
            for shape, kind in (
                (square, BF16), (square, BF16), ((heads, HEAD), F32), (square, BF16), (square, BF16),
                ((BLOCK, 16), F32), ((count, *piece), BF16), (square, F32), (square, F32),
            )
        ],
        in_specs=[pl.BlockSpec(memory_space=pltpu.HBM)] * 7,
        out_specs=[pl.BlockSpec(memory_space=pltpu.VMEM)] * 9,
        scratch_shapes=[
            vmem((heads, BLOCK), F32), vmem((heads, HEAD), F32),
            *[vmem(square, BF16)] * 3,
            vmem((16, BLOCK), F32), vmem((BLOCK, BLOCK), BF16),
            vmem((BLOCK, 16), F32), vmem((16, BLOCK), F32), vmem((BLOCK, 16), F32),
            vmem(pairs, F32), vmem(pairs, BF16), vmem(pairs, BF16),
            *[vmem(square, F32)] * 4, vmem(square, BF16), vmem((heads, 2 * HEAD, BLOCK), BF16),
            *[vmem((heads, 1, HEAD), F32)] * 3, vmem((n // 2, 1, HEAD), F32),
            vmem((2 * CHUNKS, CHUNK), F32), vmem((m, 2 * CHUNKS, CHUNK), F32),
            vmem((CHUNK, CHUNK), F32), vmem((CHUNK, CHUNK), F32),
            *[vmem((heads, HEAD), F32)] * 2, vmem((n // 2, heads, HEAD), F32),
            *sweep, vmem((count, *piece), BF16),
            *sweep,
            pltpu.SemaphoreType.DMA((7,)),
            pltpu.SemaphoreType.DMA((SEMAPHORES,)), pltpu.SemaphoreType.DMA((SEMAPHORES,)),
        ],
        compiler_params=pltpu.CompilerParams(
            collective_id=0, has_side_effects=True, vmem_limit_bytes=40 << 20
        ),
    )(*[pltpu.with_memory_space_constraint(x, pltpu.HBM) for x in (log_decay, gain.reshape(heads, HEAD), keys, values, queries, gate, grad_out)])
    dq, dgate, dgain, dk, dv = pl.pallas_call(
        finish,
        out_shape=[jax.ShapeDtypeStruct(x.shape, x.dtype) for x in (*outs[:3], *outs[:2])],
        in_specs=[pl.BlockSpec(memory_space=pltpu.VMEM)] * len(outs),
        out_specs=[pl.BlockSpec(memory_space=pltpu.HBM)] * 5,
        scratch_shapes=[*[vmem(square, BF16)] * 2, pltpu.SemaphoreType.DMA((3 + 2 * heads,))],
        compiler_params=pltpu.CompilerParams(vmem_limit_bytes=16 << 20),
    )(*[pltpu.with_memory_space_constraint(x, pltpu.VMEM) for x in outs])
    return dq, dk, dv, dgate, dgain.reshape(width)


def solution(mesh):
    return jax.shard_map(
        functools.partial(local, mesh.shape["ctx"], mesh.shape["tp"]),
        mesh=mesh,
        in_specs=(
            P("ctx", "tp"),
            P("ctx", "tp"),
            P("ctx", "tp"),
            P("tp", "ctx"),
            P("ctx", "tp"),
            P("tp"),
            P(("ctx", "tp"), None),
        ),
        out_specs=(P("ctx", "tp"), P("ctx", "tp"), P("ctx", "tp"), P("ctx", "tp"), P("tp")),
        check_vma=False,
    )
```
